256 devices in a mesh: comp: 2 (over core), gx: 32 (over x, z), gy: 4 (over y).
Axes of the slice: x: 4, y: 4, z: 8, core: 2. Of those that a mesh axis runs over, the one named last changes fastest.
Arguments:
- theta: float32 [2, 48, 1024, 512], P('comp', None, 'gx', 'gy'), may hold values from -0.5 to 1.5
- surface: float32 [2, 1024, 512], P('comp', 'gx', 'gy'), may hold values from -6 to 6
- kappa: float32 [2, 1024, 512], P('comp', 'gx', 'gy'), may hold values from 0.005 to 0.05
- depth: float32 [1024, 512], P('gx', 'gy'), may hold values from 0.2 to 1
- wet: int32 [1024, 512], P('gx', 'gy'), may hold values 0 or 1
- remap_ids: int32 [2, 256, 128, 8], P('comp', 'gx', 'gy'), may hold values from 0 to 32767, as said below
- remap_counts: int32 [2, 256, 128], P('comp', 'gx', 'gy'), may hold values from 1 to 8
- remap_weights: bfloat16 [2, 256, 128, 16, 128], P('comp', 'gx', 'gy'), may hold values from -0.5 to 0.5
Outputs:
- theta_out: float32 [2, 48, 1024, 512], P('comp', None, 'gx', 'gy')
- surface_out: float32 [2, 1024, 512], P('comp', 'gx', 'gy')
The draws below stay inside these ranges and needn't reach their ends.
Inputs may be any that keep to these rules, and one draw needn't show every extreme that they name: `remap_ids`: tiles of a component are numbered id = (device * tiles of a device) + tile, device = gx index * (devices along gy) + gy index, tile row-major over the device's 32/4 x 128/4 tiles. Every id lies on a device whose gx index is within 1 of the destination tile's device, cyclically; both distances +1 and -1 occur on every destination device. Slots at or beyond a tile's count are ignored.
All inputs are finite; a program needn't handle non-finite values. No bound on the sum of `wet` on one device may be relied on, other than what follows from the above.
Results may differ from the reference program's by a relative error of at most 0.0003.
Values sent between devices are 32-bit elements; how exact they have to be, the bound alone decides.
A program may use at most 128 MiB of HBM per device.

```python
import math
import jax
import jax.numpy as jnp
import numpy as np
from jax import lax

CX = 32
CY = 128
LEV = 48
NSTEP = 6
ITERS = 4
SLOTS = 8
REACH = 1
NX = 1024
NY = 512
N_GX = 32
N_GY = 4


def draw_remap_ids(key, part):
    tiles_lon = NX // 4
    tiles_lat = NY // 4
    lon_devices = NX // CX
    lat_devices = NY // CY
    units = CX // 4 * (CY // 4)
    shape = (2, tiles_lon, tiles_lat, SLOTS)
    offset_key = jax.random.fold_in(key, 11)
    lat_key = jax.random.fold_in(key, 12)
    unit_key = jax.random.fold_in(key, 13)
    offsets = jax.random.randint(offset_key, shape, -REACH, REACH + 1)
    tile_lon = lax.broadcasted_iota(jnp.int32, shape, 1)
    tile_lat = lax.broadcasted_iota(jnp.int32, shape, 2)
    slot = lax.broadcasted_iota(jnp.int32, shape, 3)
    first = (tile_lon % (CX // 4) == 0) & (tile_lat % (CY // 4) == 0)
    offsets = jnp.where(first & (slot == 0), REACH, jnp.where(first & (slot == 1), -REACH, offsets))
    source_lon = (tile_lon // (CX // 4) + offsets) % lon_devices
    source_lat = jax.random.randint(lat_key, shape, 0, lat_devices)
    unit = jax.random.randint(unit_key, shape, 0, units)
    return ((source_lon * lat_devices + source_lat) * units + unit).astype(jnp.int32)


def plant(drawn, own_key, low, largest):
    spot = [jax.random.randint(jax.random.fold_in(own_key, axis), (), 0, length) for axis, length in enumerate(drawn.shape)]
    widest = drawn.shape.index(max(drawn.shape))
    neighbour = spot[:widest] + [(spot[widest] + 1) % drawn.shape[widest]] + spot[widest + 1:]
    return drawn.at[tuple(spot)].set(low).at[tuple(neighbour)].set(largest)


def block_levels(own_key, dims, pieces, least, high):
    gain, own = 1.0, jax.random.fold_in(own_key, 6)
    for axis_at, shards_of in pieces:
        draws = jnp.exp(jax.random.uniform(jax.random.fold_in(own, axis_at), (shards_of,), jnp.float32, least / len(pieces), high / len(pieces)))
        gain = gain * jnp.repeat(draws, dims[axis_at] // shards_of).reshape([-1 if axis == axis_at else 1 for axis in range(len(dims))])
    return gain


def bell_draw(key, dims, spread, reach, split=(), held_as=jnp.bfloat16):
    values = jax.random.normal(key, dims, jnp.float32) * spread
    if len(split) > 0:
        values = block_levels(key, dims, split, -0.22, 0.18) * values
    return jnp.clip(values, min=-reach, max=reach).astype(held_as)


def setup_inputs(seed: int = 0) -> dict:
    keys = jax.random.split(jax.random.key(seed), 9)
    return {
        "theta": jnp.clip(-0.5 + 2.0 * jax.random.uniform(keys[0], (2, LEV, NX, NY), jnp.float32) ** block_levels(keys[0], (2, LEV, NX, NY), ((0, 2), (2, 32), (3, 4)), -0.2, 0.2), -0.5, 1.5),
        "surface": bell_draw(keys[1], (2, NX, NY), 1.0, 6.0, ((0, 2), (1, 32), (2, 4)), jnp.float32),
        "kappa": jnp.clip(jnp.exp(math.log(0.05) - 2.3025851 * jax.random.uniform(keys[2], (2, NX, NY), jnp.float32) ** block_levels(keys[2], (2, NX, NY), ((0, 2), (1, 32), (2, 4)), -0.2, 0.2)), 0.005, 0.05),
        "depth": jnp.clip(jnp.exp(math.log(1.0) - 1.609438 * jax.random.uniform(keys[3], (NX, NY), jnp.float32) ** block_levels(keys[3], (NX, NY), ((0, 32), (1, 4)), -0.2, 0.2)), 0.2, 1.0),
        "wet": plant((jax.random.randint(keys[4], (NX, NY), 0, 10) < 7).astype(jnp.int32), jax.random.fold_in(keys[4], 1), 0, 1),
        "remap_ids": draw_remap_ids(jax.random.fold_in(keys[8], 71), 0),
        "remap_counts": plant(jax.random.randint(keys[6], (2, NX // 4, NY // 4), 1, SLOTS + 1), jax.random.fold_in(keys[6], 1), 1, SLOTS).astype(jnp.int32),
        "remap_weights": bell_draw(keys[7], (2, NX // 4, NY // 4, 16, SLOTS * 16), (SLOTS * 16) ** -0.5, 0.5, ((0, 2), (1, 32), (2, 4))),
    }


node_derivative = np.array([[-3.0, 4.045084971874737, -1.545084971874737, 0.5], [-0.809016994374947, 0.0, 1.118033988749895, -0.309016994374947], [0.309016994374947, -1.118033988749895, 0.0, 0.809016994374947], [-0.5, 1.545084971874737, -4.045084971874737, 3.0]])
second_derivative = node_derivative @ node_derivative
vertical_mix = 0.2
heat_rate = 0.5
air_rate = 0.3
press_rate = 0.1
damping = 0.05
fresh_rate = 0.5
bound_low = 0.02
bound_high = 2.0

def east_of(field):
    return jnp.roll(field, -1, axis=-2)

def west_of(field):
    return jnp.roll(field, 1, axis=-2)

def north_of(field):
    return jnp.concatenate([field[..., 1:], jnp.zeros_like(field[..., :1])], axis=-1)

def south_of(field):
    return jnp.concatenate([jnp.zeros_like(field[..., :1]), field[..., :-1]], axis=-1)

def face_weights(coefficient, wet_float):
    weighted = coefficient * wet_float
    east = 0.5 * (weighted + east_of(weighted)) * wet_float * east_of(wet_float)
    north = 0.5 * (weighted + north_of(weighted)) * wet_float * north_of(wet_float)
    return (east, west_of(east), north, south_of(north))

def vertical(column):
    change = column[..., 1:, :, :] - column[..., :-1, :, :]
    zero = jnp.zeros_like(column[..., :1, :, :])
    return vertical_mix * (jnp.concatenate([change, zero], axis=-3) - jnp.concatenate([zero, change], axis=-3))

def ocean_column(column, faces, wet_float, forcing):
    east, west, north, south = faces
    flux = east * (east_of(column) - column) + west * (west_of(column) - column) + north * (north_of(column) - column) + south * (south_of(column) - column)
    result = column + flux + wet_float * vertical(column)
    return result.at[0].add(forcing)

def assemble(field):
    lon_cells, lat_cells = (field.shape[-2], field.shape[-1])
    lon_phase = lax.broadcasted_iota(jnp.int32, (lon_cells, 1), 0) % 4
    across = jnp.where(lon_phase == 0, 0.5 * (field + west_of(field)), jnp.where(lon_phase == 3, 0.5 * (field + east_of(field)), field))
    lat_place = lax.broadcasted_iota(jnp.int32, (1, lat_cells), 1)
    lower = 0.5 * (across + south_of(across))
    upper = 0.5 * (across + north_of(across))
    use_low = (lat_place % 4 == 0) & (lat_place > 0)
    use_high = (lat_place % 4 == 3) & (lat_place < lat_cells - 1)
    return jnp.where(use_low, lower, jnp.where(use_high, upper, across))

def element_laplacian(field):
    shape = field.shape
    blocks = field.reshape(shape[:-2] + (shape[-2] // 4, 4, shape[-1] // 4, 4))
    table = jnp.asarray(second_derivative, jnp.float32)
    along_lon = jnp.einsum('ij,...ajbk->...aibk', table, blocks, precision=lax.Precision.HIGHEST)
    along_lat = jnp.einsum('ij,...abkj->...abki', table, blocks, precision=lax.Precision.HIGHEST)
    return (along_lon + along_lat).reshape(shape)

def air_column(assembled, diffusivity, imported):
    result = assembled + diffusivity * element_laplacian(assembled) + vertical(assembled)
    return result.at[0].add(air_rate * (imported[0] - imported[1] * assembled[0]))

def press_update(assembled, diffusivity, imported):
    return assembled + diffusivity * element_laplacian(assembled) + press_rate * (imported[0] - assembled)

def barotropic(faces, wet_float, field):
    east, west, north, south = faces
    diagonal = damping + east + west + north + south
    neighbours = east * east_of(field) + west * west_of(field) + north * north_of(field) + south * south_of(field)
    return wet_float * (diagonal * field - neighbours) + (1.0 - wet_float) * field

def precondition(faces, wet_float, residual):
    east, west, north, south = faces
    diagonal = damping + east + west + north + south
    lon_cells, lat_cells = residual.shape
    lat_place = lax.broadcasted_iota(jnp.int32, residual.shape, 1) % CY
    main = wet_float * diagonal + (1.0 - wet_float)
    lower = jnp.where(lat_place == 0, 0.0, -south)
    upper = jnp.where(lat_place == CY - 1, 0.0, -north)
    line_shape = (lon_cells, lat_cells // CY, CY)
    solved = lax.linalg.tridiagonal_solve(lower.reshape(line_shape), main.reshape(line_shape), upper.reshape(line_shape), residual.reshape(line_shape)[..., None])
    return solved[..., 0].reshape(lon_cells, lat_cells)

def remap(source, source_ids, counts, weights):
    channels = source.shape[0]
    tiles_lon, tiles_lat = (source_ids.shape[0], source_ids.shape[1])
    table = source.reshape(channels, N_GX, CX // 4, 4, N_GY, CY // 4, 4).transpose(1, 4, 2, 5, 0, 3, 6).reshape(-1, channels, 16)
    picked = table[source_ids]
    slot = lax.broadcasted_iota(jnp.int32, source_ids.shape, 2)
    valid = (slot < counts[..., None]).astype(jnp.float32)
    masked = weights.astype(jnp.float32).reshape(tiles_lon, tiles_lat, 16, SLOTS, 16) * valid[:, :, None, :, None]
    mapped = jnp.einsum('abcms,abmfs->abfc', masked, picked, precision=lax.Precision.HIGHEST)
    return mapped.reshape(tiles_lon, tiles_lat, channels, 4, 4).transpose(2, 0, 3, 1, 4).reshape(channels, tiles_lon * 4, tiles_lat * 4)

def reference(theta, surface, kappa, depth, wet, remap_ids, remap_counts, remap_weights):
    wet_float = wet.astype(jnp.float32)
    ocean = theta[0]
    air = theta[1]
    ocean_export = jnp.stack([ocean[0] * wet_float, wet_float])
    air_export = jnp.stack([air[0], surface[1]])
    to_ocean = remap(air_export, remap_ids[0], remap_counts[0], remap_weights[0])
    to_air = remap(ocean_export, remap_ids[1], remap_counts[1], remap_weights[1])
    sent = jnp.sum(air[0])
    received = jnp.sum(wet_float * to_ocean[0])
    wet_total = jnp.sum(wet_float)
    correction = (sent - received) / wet_total
    ocean_faces = face_weights(kappa[0], wet_float)
    forcing = heat_rate * wet_float * (to_ocean[0] + correction)
    for step in range(NSTEP):
        ocean = ocean_column(ocean, ocean_faces, wet_float, forcing)
        air = air_column(assemble(air), kappa[1], to_air)
    depth_faces = face_weights(depth, wet_float)
    centre = (bound_high + bound_low) / 2.0
    half_range = (bound_high - bound_low) / 2.0
    spread_ratio = centre / half_range
    eta = surface[0]
    press = surface[1]
    right = wet_float * (damping * eta + fresh_rate * to_ocean[1])
    residual = right - barotropic(depth_faces, wet_float, eta)
    direction = precondition(depth_faces, wet_float, residual) / centre
    recurrence = 1.0 / spread_ratio
    eta = eta + direction
    press = press_update(assemble(press), kappa[1], to_air)
    for step in range(1, ITERS):
        residual = residual - barotropic(depth_faces, wet_float, direction)
        recurrence_next = 1.0 / (2.0 * spread_ratio - recurrence)
        direction = recurrence_next * recurrence * direction + 2.0 * recurrence_next / half_range * precondition(depth_faces, wet_float, residual)
        recurrence = recurrence_next
        eta = eta + direction
        press = press_update(assemble(press), kappa[1], to_air)
    return (jnp.stack([ocean, air]), jnp.stack([eta, press]))
```

```python
import functools

import jax
import jax.numpy as jnp
import ml_dtypes
import numpy as np
from jax import lax
from jax.experimental import pallas as pl
from jax.experimental.pallas import tpu as pltpu
from jax.sharding import PartitionSpec as P

MESH = pl.DeviceIdType.MESH
F32 = jnp.float32
BF16 = jnp.bfloat16

NSTEP = 6
ITERS = 4
SLOTS = 8
LEV = 48
CX = 32
CY = 128
ROWS = 56
SURF = 48

node_derivative = np.array(
    [
        [-3.0, 4.045084971874737, -1.545084971874737, 0.5],
        [-0.809016994374947, 0.0, 1.118033988749895, -0.309016994374947],
        [0.309016994374947, -1.118033988749895, 0.0, 0.809016994374947],
        [-0.5, 1.545084971874737, -4.045084971874737, 3.0],
    ]
)
second_derivative = node_derivative @ node_derivative
vertical_mix = 0.2
heat_rate = 0.5
air_rate = 0.3
press_rate = 0.1
damping = 0.05
fresh_rate = 0.5
bound_low = 0.02
bound_high = 2.0


def heat_response():
    level = np.zeros(LEV)
    for _ in range(NSTEP):
        change = level[1:] - level[:-1]
        level = level + vertical_mix * (np.append(change, 0.0) - np.append(0.0, change))
        level[0] += heat_rate
    return [float(v) for v in level]


def halves(table):
    high = table.astype(ml_dtypes.bfloat16)
    low = (table - high.astype(np.float64)).astype(ml_dtypes.bfloat16)
    return high, low


def tables():
    lane = np.arange(256)
    f_in, dx_in, dy_in = (lane // 64) % 2, (lane // 16) % 4, lane % 4
    f_out, dx_out, dy_out = lane // 128, (lane // 4) % 4, lane % 4
    fold = (
        (f_in[:, None] == f_out[None])
        & (dx_in[:, None] == dx_out[None])
        & (dy_in[:, None] == dy_out[None])
    )
    block = np.kron(np.eye(32), second_derivative.T)
    high, low = halves(block)
    zero = np.zeros((128, 128))
    lap = np.block(
        [[high.astype(np.float64), low.astype(np.float64)], [high.astype(np.float64), zero]]
    )
    lane = np.arange(128)
    target = ((lane // 4) % 4) * 32 + (lane // 16) * 4 + lane % 4
    perm = np.zeros((128, 256))
    perm[lane, target] = 1.0
    return np.concatenate([fold.astype(np.float64), lap, perm]).astype(ml_dtypes.bfloat16)


def split(value):
    high = value.astype(BF16)
    low = (value - high.astype(F32)).astype(BF16)
    return high, low


def dot(a, b):
    return jnp.dot(a, b, preferred_element_type=F32)


def radices(count):
    if count == 32:
        return [4, 2, 4]
    found = []
    while count > 1:
        size = 4 if count % 4 == 0 else count
        found.append(size)
        count //= size
    return found


def kernel(
    n_gx,
    n_gy,
    theta,
    surface,
    kappa,
    depth,
    wet,
    ids,
    counts,
    weights,
    consts,
    theta_out,
    surface_out,
    fp,
    ys,
    yr,
    zb,
    ex,
    tsend,
    trecv,
    table,
    wbuf,
    cbuf,
    idbuf,
    cntbuf,
    wetbuf,
    coef,
    pb,
    dbuf,
    imp,
    pcr,
    grid,
    red,
    redr,
    lsem,
    hs,
    hr,
    es,
    er,
    rs,
    rr,
):
    comp = lax.axis_index("comp")
    gx = lax.axis_index("gx")
    gy = lax.axis_index("gy")
    sources = 3 * n_gy
    units = (CX // 4) * (CY // 4)
    is_ocean = comp == 0
    is_air = comp == 1
    has_south = gy > 0
    has_north = gy < n_gy - 1

    def place(dc, dx, dy):
        return (lax.rem(comp + dc, 2), lax.rem(gx + dx + n_gx, n_gx), lax.rem(gy + dy + n_gy, n_gy))

    halo_peers = [
        place(0, 1, 0),
        place(0, -1, 0),
        place(0, 0, 1),
        place(0, 0, -1),
        place(0, 1, 1),
        place(0, -1, 1),
        place(0, 1, -1),
        place(0, -1, -1),
    ]
    export_peers = [(d, j, place(1, d, j)) for d in (-1, 0, 1) for j in range(n_gy)]
    sum_phases = []
    sum_phases.append([place(dc, 0, j) for dc in range(2) for j in range(n_gy) if dc or j])
    stride = 1
    for size in radices(n_gx):
        digit = lax.rem(gx // stride, size)
        group = []
        for j in range(1, size):
            group.append((comp, gx + (lax.rem(digit + j, size) - digit) * stride, gy))
        sum_phases.append(group)
        stride *= size

    loads = {}

    def load(name, index, src, dst):
        copy = pltpu.make_async_copy(src, dst, lsem.at[index])
        copy.start()
        loads.setdefault(name, []).append(copy)

    def loaded(name):
        for copy in loads.pop(name):
            copy.wait()

    load("export", 0, theta.at[0, 0], grid.at[0])
    load("export", 1, surface.at[0], grid.at[1])
    load("export", 2, wet, wetbuf)
    load("export", 3, kappa.at[0], grid.at[2])
    load("export", 4, depth, grid.at[3])
    for x in range(CX):
        load("theta", 8 + x, theta.at[0, :, x, :], fp.at[0, x + 1, pl.ds(0, LEV), :])
    load("remap", 5, ids.at[0], idbuf)
    load("remap", 6, counts.at[0], cntbuf)
    load("tables", 7, consts, cbuf)
    load("weights", 40, weights.at[0], wbuf)

    barrier = pltpu.get_barrier_semaphore()
    greeted = halo_peers + [p for _, _, p in export_peers] + [p for g in sum_phases for p in g]
    for peer in greeted:
        pl.semaphore_signal(barrier, inc=1, device_id=peer, device_id_type=MESH)

    lane128 = lax.broadcasted_iota(jnp.int32, (8, 128), 1)
    lane1 = lax.broadcasted_iota(jnp.int32, (1, 128), 1)

    loaded("export")
    wet_float = wetbuf[...].astype(F32)
    grid[4] = wet_float
    top = grid[0]

    ex[0] = jnp.where(is_ocean, top * wet_float, top)
    ex[1] = jnp.where(is_ocean, wet_float, grid[1])
    parts = [ex[f, pl.ds(dx, 8, stride=4), :] for f in range(2) for dx in range(4)]
    for h in range(8):
        acc = jnp.zeros((8, 128), F32)
        for j in range(8):
            shift = ((j - h) * 16) % 128
            moved = pltpu.roll(parts[j], shift, 1) if shift else parts[j]
            acc = jnp.where(lane128 // 16 == j, moved, acc)
        tsend[pl.ds(8 * h, 8), :] = acc

    for x in range(CX):
        fp[0, x + 1, SURF : SURF + 1, :] = grid[1, x : x + 1, :]
        fp[0, x + 1, SURF + 1 : SURF + 2, :] = grid[2, x : x + 1, :]
        fp[0, x + 1, SURF + 2 : SURF + 3, :] = grid[3, x : x + 1, :]
        fp[0, x + 1, SURF + 3 : SURF + 4, :] = grid[4, x : x + 1, :]
        fp[0, x + 1, SURF + 4 : SURF + 8, :] = jnp.zeros((4, 128), F32)

    def pack(s):
        def body(x, accs):
            accs = list(accs)
            for b in range(7):
                base = 2 * x + 64 * (b % 2)
                moved = pltpu.roll(fp[s, x + 1, 8 * b : 8 * b + 8, :], base + 1, 1)
                accs[b // 2] = jnp.where(
                    (lane128 == base) | (lane128 == base + 1), moved, accs[b // 2]
                )
            return tuple(accs)

        zero = jnp.zeros((8, 128), F32)
        accs = lax.fori_loop(0, CX, body, (zero,) * 4)
        for j in range(4):
            ys[s, j] = accs[j]

    def copy_to(s, d):
        if d == 0:
            src, dst, peer = fp.at[s, CX], fp.at[s, 0], halo_peers[0]
        elif d == 1:
            src, dst, peer = fp.at[s, 1], fp.at[s, CX + 1], halo_peers[1]
        else:
            src, dst, peer = ys.at[s], yr.at[s, d - 2], halo_peers[d]
        return pltpu.make_async_remote_copy(
            src_ref=src,
            dst_ref=dst,
            send_sem=hs.at[s, d],
            recv_sem=hr.at[s, d],
            device_id=peer,
            device_id_type=MESH,
        )

    def send_halo(s):
        for d in range(4):
            copy_to(s, d).start()

        @pl.when(is_air)
        def _():
            for d in range(4, 8):
                copy_to(s, d).start()

    def wait_halo(s):
        for d in range(4):
            copy_to(s, d).wait_recv()

        @pl.when(is_air)
        def _():
            for d in range(4, 8):
                copy_to(s, d).wait_recv()

    def drain_halo(s):
        for d in range(4):
            copy_to(s, d).wait_send()

        @pl.when(is_air)
        def _():
            for d in range(4, 8):
                copy_to(s, d).wait_send()

    def merged(s, south, north):
        found = []
        for j in range(4):
            low = yr[s, south, j]
            high = pltpu.roll(yr[s, north, j], 126, 1)
            found.append(jnp.where(lane128 % 2 == 0, low, high))
        return found

    def unpack(s, corners):
        own = merged(s, 0, 1)

        def fill(x, vectors, slab):
            for b in range(7):
                shift = lax.rem(256 - 2 * x - 64 * (b % 2), 128)
                zb[slab, 8 * b : 8 * b + 8, :] = pltpu.roll(vectors[b // 2], shift, 1)

        def body(x, carry):
            fill(x, own, x + 1)
            return carry

        lax.fori_loop(0, CX, body, 0)
        if corners:
            fill(CX - 1, merged(s, 2, 4), 0)
            fill(0, merged(s, 3, 5), CX + 1)

    def export_copy(d, j, peer):
        slot = (1 - d) * n_gy + gy
        return pltpu.make_async_remote_copy(
            src_ref=tsend,
            dst_ref=trecv.at[slot],
            send_sem=es.at[(d + 1) * n_gy + j],
            recv_sem=er.at[slot],
            device_id=peer,
            device_id_type=MESH,
        )

    loaded("theta")
    pack(0)
    pl.semaphore_wait(barrier, len(greeted))
    for d, j, peer in export_peers:
        export_copy(d, j, peer).start()
    send_halo(0)

    loaded("remap")
    loaded("tables")
    cnt = cntbuf[...].astype(F32)
    lane32 = lax.broadcasted_iota(jnp.int32, (32, 32), 1)
    row32 = lax.broadcasted_iota(jnp.int32, (32, 32), 0)
    ones = jnp.ones((32, 128), BF16)
    counted = []
    for tx in range(8):
        spread = jnp.where(lane32 == row32, jnp.broadcast_to(cnt[tx : tx + 1, :], (32, 32)), 0.0)
        counted.append(dot(spread.astype(BF16), ones)[:, :SLOTS])
    counted = jnp.concatenate(counted, axis=0)
    id_all = idbuf[...].reshape(units, SLOTS)
    slot_lane = lax.broadcasted_iota(jnp.int32, (units, SLOTS), 1)
    dev = id_all // units
    unit = id_all - dev * units
    dev_gx = dev // n_gy
    dev_gy = dev - dev_gx * n_gy
    tile_x = unit // 32
    tile_y = unit - tile_x * 32
    offset = dev_gx - gx + 1
    offset = jnp.where(offset < 0, offset + n_gx, jnp.where(offset >= n_gx, offset - n_gx, offset))
    key = (offset * n_gy + dev_gy) * 64 + (tile_y // 4) * 8 + tile_x
    key = jnp.where(slot_lane.astype(F32) < counted, key, -1)
    tile_low = tile_y - (tile_y // 4) * 4

    wait_halo(0)
    unpack(0, True)

    def rims(s, row):
        pass

    def lanes_of(shape):
        return lax.broadcasted_iota(jnp.int32, shape, 1)

    lane_full = lanes_of((CX, CY))

    def gather_row(s, row, slot):
        for x in range(CX):
            grid[slot, x : x + 1, :] = fp[s, x + 1, row : row + 1, :]

    def rim_row(row, slot):
        for x in range(CX):
            grid[slot, x : x + 1, :] = zb[x + 1, row : row + 1, :]

    def shifted(center, west_row, east_row, rim):
        row_place = lax.broadcasted_iota(jnp.int32, (CX, CY), 0)
        east = jnp.where(row_place == CX - 1, east_row, pltpu.roll(center, CX - 1, 0))
        west = jnp.where(row_place == 0, west_row, pltpu.roll(center, 1, 0))
        north = jnp.where(lane_full == CY - 1, rim, pltpu.roll(center, CY - 1, 1))
        south = jnp.where(lane_full == 0, rim, pltpu.roll(center, 1, 1))
        return east, west, north, south

    def side_rows(s, row):
        return fp[s, 0, row : row + 1, :], fp[s, CX + 1, row : row + 1, :]

    @pl.when(is_ocean)
    def _():
        wet_c = grid[4]
        rim_row(SURF + 3, 5)
        we, ww, wn, ws = shifted(wet_c, *side_rows(0, SURF + 3), grid[5])
        wn = jnp.where((lane_full == CY - 1) & jnp.logical_not(has_north), 0.0, wn)
        ws = jnp.where((lane_full == 0) & jnp.logical_not(has_south), 0.0, ws)
        for row, slot, at in ((SURF + 1, 2, 0), (SURF + 2, 3, 6)):
            center = grid[slot]
            rim_row(row, 5)
            ke, kw, kn, ks = shifted(center, *side_rows(0, row), grid[5])
            base = center * wet_c
            coef[at] = 0.5 * (base + ke * we) * wet_c * we
            coef[at + 1] = 0.5 * (kw * ww + base) * ww * wet_c
            coef[at + 2] = 0.5 * (base + kn * wn) * wet_c * wn
            coef[at + 3] = 0.5 * (ks * ws + base) * ws * wet_c
        coef[4] = (
            1.0 - (coef[0] + coef[1] + coef[2] + coef[3]) - (2.0 * vertical_mix) * wet_c
        )
        coef[5] = vertical_mix * wet_c
        diagonal = damping + coef[6] + coef[7] + coef[8] + coef[9]
        coef[10] = diagonal
        main = wet_c * diagonal + (1.0 - wet_c)
        lower = jnp.where(lane_full == 0, 0.0, -coef[9])
        upper = jnp.where(lane_full == CY - 1, 0.0, -coef[8])
        step = 1
        index = 0
        while step < CY:
            back = CY - step
            below_main = pltpu.roll(main, step, 1)
            above_main = pltpu.roll(main, back, 1)
            factor_below = -lower / below_main
            factor_above = -upper / above_main
            pcr[index] = factor_below
            pcr[index + 1] = factor_above
            main = (
                main
                + factor_below * pltpu.roll(upper, step, 1)
                + factor_above * pltpu.roll(lower, back, 1)
            )
            lower = factor_below * pltpu.roll(lower, step, 1)
            upper = factor_above * pltpu.roll(upper, back, 1)
            step *= 2
            index += 2
        pcr[14] = 1.0 / main

    def solve(values):
        step = 1
        index = 0
        while step < CY:
            values = (
                values
                + pcr[index] * pltpu.roll(values, step, 1)
                + pcr[index + 1] * pltpu.roll(values, CY - step, 1)
            )
            step *= 2
            index += 2
        return values * pcr[14]

    lane56 = lanes_of((ROWS, CY))
    row56 = lax.broadcasted_iota(jnp.int32, (ROWS, CY), 0)
    row48 = lax.broadcasted_iota(jnp.int32, (LEV, CY), 0)
    lane48 = lanes_of((LEV, CY))

    def ocean_step(s):
        def body(x, carry):
            c = fp[s - 1, x + 1, 0:LEV, :]
            w = fp[s - 1, x, 0:LEV, :]
            e = fp[s - 1, x + 2, 0:LEV, :]
            z = zb[x + 1, 0:LEV, :]

            def row(i):
                return coef[i, pl.ds(x, 1), :]

            n = jnp.where(lane48 == CY - 1, z, pltpu.roll(c, CY - 1, 1))
            o = jnp.where(lane48 == 0, z, pltpu.roll(c, 1, 1))
            up = jnp.where(row48 == LEV - 1, c, pltpu.roll(c, LEV - 1, 0))
            down = jnp.where(row48 == 0, c, pltpu.roll(c, 1, 0))
            new = (
                row(4) * c
                + row(0) * e
                + row(1) * w
                + row(2) * n
                + row(3) * o
                + row(5) * (up + down)
            )
            fp[s, x + 1, 0:LEV, :] = new
            if s > 1:
                fp[s, x + 1, 0:1, :] = new[0:1, :] + grid[7, pl.ds(x, 1), :]
            return carry

        lax.fori_loop(0, CX, body, 0)

    def air_step(s):
        h = jnp.where(
            ((lane1 % 4 == 0) & ((lane1 > 0) | has_south))
            | ((lane1 % 4 == 3) & ((lane1 < CY - 1) | has_north)),
            0.5,
            0.0,
        )
        mix_up = jnp.where(row56 < LEV - 1, vertical_mix, 0.0)
        mix_down = jnp.where((row56 > 0) & (row56 < LEV), vertical_mix, 0.0)

        def body(i, carry):
            x0 = 4 * i
            v = [fp[s - 1, x0 + j] for j in range(6)]
            z = [zb[x0 + j] for j in range(6)]

            def across(t):
                return [0.5 * (t[1] + t[0]), t[2], t[3], 0.5 * (t[4] + t[5])]

            blocks = []
            for a, za in zip(across(v), across(z)):
                partner = jnp.where(lane56 % 4 == 0, pltpu.roll(a, 1, 1), pltpu.roll(a, CY - 1, 1))
                partner = jnp.where((lane56 == 0) | (lane56 == CY - 1), za, partner)
                blocks.append(a + h * (partner - a))
            high, low = split(jnp.concatenate(blocks, axis=0))
            along = dot(jnp.concatenate([high, low], axis=1), cbuf[256:512, :])
            along = along[:, :CY] + along[:, CY:]
            for j in range(4):
                b = blocks[j]
                lap = along[ROWS * j : ROWS * (j + 1)]
                for m in range(4):
                    lap = lap + float(second_derivative[j, m]) * blocks[m]
                up = pltpu.roll(b, ROWS - 1, 0)
                down = pltpu.roll(b, 1, 0)
                new = (
                    b
                    + grid[2, pl.ds(x0 + j, 1), :] * lap
                    + mix_up * (up - b)
                    + mix_down * (down - b)
                )
                x = x0 + j
                fp[s, x + 1] = new
                if s == 1:
                    grid[8, pl.ds(x, 1), :] = b[0:1, :]
                    grid[9, pl.ds(x, 1), :] = b[SURF : SURF + 1, :]
                else:
                    fp[s, x + 1, 0:1, :] = (
                        new[0:1, :]
                        + grid[6, pl.ds(x, 1), :]
                        - grid[7, pl.ds(x, 1), :] * b[0:1, :]
                    )
                    if s <= ITERS:
                        fp[s, x + 1, SURF : SURF + 1, :] = (
                            new[SURF : SURF + 1, :]
                            + grid[10, pl.ds(x, 1), :]
                            - press_rate * b[SURF : SURF + 1, :]
                        )
            return carry

        lax.fori_loop(0, CX // 4, body, 0)

    def forward(s):
        @pl.when(is_ocean)
        def _():
            ocean_step(s)

        @pl.when(is_air)
        def _():
            air_step(s)

    forward(1)

    for d in range(3):
        for j in range(n_gy):
            slot = d * n_gy + j
            pltpu.make_async_remote_copy(
                src_ref=tsend,
                dst_ref=trecv.at[slot],
                send_sem=es.at[slot],
                recv_sem=er.at[slot],
                device_id=halo_peers[0],
                device_id_type=MESH,
            ).wait_recv()
    high, low = split(trecv[...].reshape(sources * 64, 128))
    table[:, 0:128] = high
    table[:, 128:256] = low
    key_lane = lax.broadcasted_iota(jnp.int32, (units, sources * 64), 1)
    lane256 = lax.broadcasted_iota(jnp.int32, (units, 256), 1)
    low_lane = (lane256 // 4) % 4
    slot_of = (lane256 // 16) % 8
    picked = jnp.zeros((units, 256), F32)
    for m in range(SLOTS):
        hot = jnp.where(key[:, m : m + 1] == key_lane, 1.0, 0.0).astype(BF16)
        found = dot(hot, table[...])
        found = jnp.where(low_lane == tile_low[:, m : m + 1], found, 0.0).astype(BF16)
        picked = jnp.where(slot_of == m, dot(found, cbuf[0:256, :]), picked)
    high, low = split(picked)
    pb[0] = high[:, 0:128]
    pb[1] = high[:, 128:256]
    pb[2] = low[:, 0:128]
    pb[3] = low[:, 128:256]
    loaded("weights")
    own_tile = lax.broadcasted_iota(jnp.int32, (16, 256), 0) == (
        lax.broadcasted_iota(jnp.int32, (16, 256), 1) // 16
    )
    for g in range(16):
        left = pb[:, 16 * g : 16 * g + 16, :].reshape(64, 128)
        right = wbuf[g // 2, 16 * (g % 2) : 16 * (g % 2) + 16].reshape(256, 128)
        out = lax.dot_general(
            left, right, (((1,), (1,)), ((), ())), preferred_element_type=F32
        )
        for f in range(2):
            value = out[16 * f : 16 * f + 16] + out[32 + 16 * f : 48 + 16 * f]
            value = jnp.sum(jnp.where(own_tile, value, 0.0), axis=0, keepdims=True)
            for u in range(2):
                dbuf[f, 2 * (g % 2) + u, g // 2 : g // 2 + 1, :] = value[:, 128 * u : 128 * u + 128]
    high, low = split(dbuf[...].reshape(64, 128))
    turned = dot(jnp.concatenate([high, low], axis=0), cbuf[512:640, 0:128])
    turned = turned[:64] + turned[64:]
    for f in range(2):
        quarters = [turned[32 * f + 8 * q : 32 * f + 8 * q + 8] for q in range(4)]
        for dx in range(4):
            acc = jnp.zeros((8, 128), F32)
            for q in range(4):
                shift = ((q - dx) * 32) % 128
                moved = pltpu.roll(quarters[q], shift, 1) if shift else quarters[q]
                acc = jnp.where(lane128 // 32 == q, moved, acc)
            imp[f, pl.ds(dx, 8, stride=4), :] = acc

    wet_c = grid[4]
    heat = jnp.where(is_ocean, -(wet_c * imp[0]), grid[0])
    cells = jnp.where(is_ocean, wet_c, 0.0)
    row8 = lax.broadcasted_iota(jnp.int32, (8, 128), 0)

    def rows8(v):
        return jnp.sum(v, axis=0, keepdims=True)

    red[0] = jnp.where(row8 == 0, rows8(heat), jnp.where(row8 == 1, rows8(cells), 0.0))

    def sum_copy(phase, j):
        return pltpu.make_async_remote_copy(
            src_ref=red.at[phase],
            dst_ref=redr.at[phase, j],
            send_sem=rs.at[phase, j],
            recv_sem=rr.at[phase, j],
            device_id=sum_phases[phase][j],
            device_id_type=MESH,
        )

    def sum_send(phase):
        for j in range(len(sum_phases[phase])):
            sum_copy(phase, j).start()

    def sum_finish(phase):
        total = red[phase]
        for j in range(len(sum_phases[phase])):
            sum_copy(phase, j).wait_recv()
            total = total + redr[phase, j]
        red[phase + 1] = total

    sum_send(0)

    centre = (bound_high + bound_low) / 2.0
    half_range = (bound_high - bound_low) / 2.0
    spread_ratio = centre / half_range

    def apply_a(s, center):
        rim_row(SURF, 5)
        east, west, north, south = shifted(center, *side_rows(s, SURF), grid[5])
        near = coef[6] * east + coef[7] * west + coef[8] * north + coef[9] * south
        return wet_c * (coef[10] * center - near) + (1.0 - wet_c) * center

    def put_surface(s, value):
        grid[13] = value
        for x in range(CX):
            fp[s, x + 1, SURF : SURF + 1, :] = grid[13, x : x + 1, :]

    @pl.when(is_ocean)
    def _():
        force = heat_rate * wet_c * imp[0]
        grid[7] = force
        for x in range(CX):
            fp[1, x + 1, 0:1, :] = fp[1, x + 1, 0:1, :] + grid[7, x : x + 1, :]
        eta = grid[1]
        residual = wet_c * (damping * eta + fresh_rate * imp[1]) - apply_a(0, eta)
        direction = solve(residual) / centre
        grid[11] = eta + direction
        grid[12] = residual
        put_surface(1, direction)

    @pl.when(is_air)
    def _():
        grid[6] = air_rate * imp[0]
        grid[7] = air_rate * imp[1]
        grid[10] = press_rate * imp[0]
        grid[5] = grid[6] - grid[7] * grid[8]
        grid[11] = grid[10] - press_rate * grid[9]
        for x in range(CX):
            fp[1, x + 1, 0:1, :] = fp[1, x + 1, 0:1, :] + grid[5, x : x + 1, :]
            fp[1, x + 1, SURF : SURF + 1, :] = (
                fp[1, x + 1, SURF : SURF + 1, :] + grid[11, x : x + 1, :]
            )

    recurrence = 1.0 / spread_ratio
    phases = len(sum_phases)
    for s in range(2, NSTEP + 1):
        pack(s - 1)
        send_halo(s - 1)
        if s - 2 >= 1 and s - 2 < phases:
            sum_send(s - 2)
        wait_halo(s - 1)
        if s - 2 < phases:
            sum_finish(s - 2)
        unpack(s - 1, True)
        forward(s)
        if s <= ITERS:
            recurrence_next = 1.0 / (2.0 * spread_ratio - recurrence)

            @pl.when(is_ocean)
            def _(s=s, recurrence=recurrence, recurrence_next=recurrence_next):
                old = grid[13]
                residual = grid[12] - apply_a(s - 1, old)
                direction = (recurrence_next * recurrence) * old + (
                    2.0 * recurrence_next / half_range
                ) * solve(residual)
                grid[11] = grid[11] + direction
                grid[12] = residual
                put_surface(s, direction)

            recurrence = recurrence_next
        if s == ITERS:

            @pl.when(is_air)
            def _(s=s):
                gather_row(s, SURF, 11)

            loads["surface"] = [pltpu.make_async_copy(grid.at[11], surface_out.at[0], lsem.at[41])]
            loads["surface"][0].start()

    total = red[phases]
    correction = jnp.sum(total[0:1, :], axis=1, keepdims=True) / jnp.sum(
        total[1:2, :], axis=1, keepdims=True
    )
    response = heat_response()

    @pl.when(is_ocean)
    def _():
        spread = jnp.zeros((8, 128), F32)
        for k in range(NSTEP):
            spread = jnp.where(row8 == k, response[k], spread)
        spread = spread * correction

        def body(x, carry):
            fp[NSTEP, x + 1, 0:8, :] = (
                fp[NSTEP, x + 1, 0:8, :] + spread * grid[4, pl.ds(x, 1), :]
            )
            return carry

        lax.fori_loop(0, CX, body, 0)

    stores = []
    for x in range(CX):
        copy = pltpu.make_async_copy(
            fp.at[NSTEP, x + 1, pl.ds(0, LEV), :], theta_out.at[0, :, x, :], lsem.at[8 + x]
        )
        copy.start()
        stores.append(copy)
    for s in range(NSTEP):
        drain_halo(s)
    for d, j, peer in export_peers:
        export_copy(d, j, peer).wait_send()
    for phase in range(phases):
        for j in range(len(sum_phases[phase])):
            sum_copy(phase, j).wait_send()
    loaded("surface")
    for copy in stores:
        copy.wait()


def solution(mesh):
    n_gx = mesh.shape["gx"]
    n_gy = mesh.shape["gy"]
    sources = 3 * n_gy
    phases = 1 + len(radices(n_gx))
    widest = max(2 * n_gy - 1, 3)
    constants = tables()

    def per_device(theta, surface, kappa, depth, wet, ids, counts, weights):
        spec = pl.BlockSpec(memory_space=pl.ANY)
        dma = pltpu.SemaphoreType.DMA
        return pl.pallas_call(
            functools.partial(kernel, n_gx, n_gy),
            out_shape=(
                jax.ShapeDtypeStruct((1, LEV, CX, CY), F32),
                jax.ShapeDtypeStruct((1, CX, CY), F32),
            ),
            in_specs=[spec] * 9,
            out_specs=(spec, spec),
            scratch_shapes=[
                pltpu.VMEM((NSTEP + 1, CX + 2, ROWS, CY), F32),
                pltpu.VMEM((NSTEP, 4, 8, CY), F32),
                pltpu.VMEM((NSTEP, 6, 4, 8, CY), F32),
                pltpu.VMEM((CX + 2, ROWS, CY), F32),
                pltpu.VMEM((2, CX, CY), F32),
                pltpu.VMEM((64, 128), F32),
                pltpu.VMEM((sources, 64, 128), F32),
                pltpu.VMEM((sources * 64, 256), BF16),
                pltpu.VMEM((8, 32, 16, 128), BF16),
                pltpu.VMEM((640, 256), BF16),
                pltpu.VMEM((8, 32, SLOTS), jnp.int32),
                pltpu.VMEM((8, 32), jnp.int32),
                pltpu.VMEM((CX, CY), jnp.int32),
                pltpu.VMEM((11, CX, CY), F32),
                pltpu.VMEM((4, 256, 128), BF16),
                pltpu.VMEM((2, 4, 8, 128), F32),
                pltpu.VMEM((2, CX, CY), F32),
                pltpu.VMEM((15, CX, CY), F32),
                pltpu.VMEM((14, CX, CY), F32),
                pltpu.VMEM((phases + 1, 8, 128), F32),
                pltpu.VMEM((phases, widest, 8, 128), F32),
                dma((42,)),
                dma((NSTEP, 8)),
                dma((NSTEP, 8)),
                dma((sources,)),
                dma((sources,)),
                dma((phases, widest)),
                dma((phases, widest)),
            ],
            compiler_params=pltpu.CompilerParams(
                collective_id=0, has_side_effects=True, vmem_limit_bytes=60 * 1024 * 1024
            ),
        )(theta, surface, kappa, depth, wet, ids, counts, weights, jnp.asarray(constants))

    in_specs = (
        P("comp", None, "gx", "gy"),
        P("comp", "gx", "gy"),
        P("comp", "gx", "gy"),
        P("gx", "gy"),
        P("gx", "gy"),
        P("comp", "gx", "gy", None),
        P("comp", "gx", "gy"),
        P("comp", "gx", "gy", None, None),
    )
    out_specs = (P("comp", None, "gx", "gy"), P("comp", "gx", "gy"))
    return jax.shard_map(
        per_device, mesh=mesh, in_specs=in_specs, out_specs=out_specs, check_vma=False
    )
```

```python
import functools

import jax
import jax.numpy as jnp
import ml_dtypes
import numpy as np
from jax import lax
from jax.experimental import pallas as pl
from jax.experimental.pallas import tpu as pltpu
from jax.sharding import PartitionSpec as P

MESH = pl.DeviceIdType.MESH
F32 = jnp.float32
BF16 = jnp.bfloat16

NSTEP = 6
ITERS = 4
SLOTS = 8
LEV = 48
CX = 32
CY = 128
ROWS = 56
SURF = 48
PACK = 32
UNPACK = 32
OCEAN = 16
AIR = 4

node_derivative = np.array(
    [
        [-3.0, 4.045084971874737, -1.545084971874737, 0.5],
        [-0.809016994374947, 0.0, 1.118033988749895, -0.309016994374947],
        [0.309016994374947, -1.118033988749895, 0.0, 0.809016994374947],
        [-0.5, 1.545084971874737, -4.045084971874737, 3.0],
    ]
)
second_derivative = node_derivative @ node_derivative
vertical_mix = 0.2
heat_rate = 0.5
air_rate = 0.3
press_rate = 0.1
damping = 0.05
fresh_rate = 0.5
bound_low = 0.02
bound_high = 2.0


def heat_response():
    level = np.zeros(LEV)
    for _ in range(NSTEP):
        change = level[1:] - level[:-1]
        level = level + vertical_mix * (np.append(change, 0.0) - np.append(0.0, change))
        level[0] += heat_rate
    return [float(v) for v in level]


def halves(table):
    high = table.astype(ml_dtypes.bfloat16)
    low = (table - high.astype(np.float64)).astype(ml_dtypes.bfloat16)
    return high, low


def tables():
    lane = np.arange(256)
    f_in, dx_in, dy_in = (lane // 64) % 2, (lane // 16) % 4, lane % 4
    f_out, dx_out, dy_out = lane // 128, (lane // 4) % 4, lane % 4
    fold = (
        (f_in[:, None] == f_out[None])
        & (dx_in[:, None] == dx_out[None])
        & (dy_in[:, None] == dy_out[None])
    )
    block = np.kron(np.eye(32), second_derivative.T)
    high, low = halves(block)
    zero = np.zeros((128, 128))
    lap = np.block(
        [[high.astype(np.float64), low.astype(np.float64)], [high.astype(np.float64), zero]]
    )
    lane = np.arange(128)
    target = ((lane // 4) % 4) * 32 + (lane // 16) * 4 + lane % 4
    perm = np.zeros((128, 256))
    perm[lane, target] = 1.0
    return np.concatenate([fold.astype(np.float64), lap, perm]).astype(ml_dtypes.bfloat16)


def split(value):
    high = value.astype(BF16)
    low = (value - high.astype(F32)).astype(BF16)
    return high, low


def dot(a, b):
    return jnp.dot(a, b, preferred_element_type=F32)


def radices(count):
    if count == 32:
        return [4, 2, 4]
    found = []
    while count > 1:
        size = 4 if count % 4 == 0 else count
        found.append(size)
        count //= size
    return found


def kernel(
    n_gx,
    n_gy,
    theta,
    surface,
    kappa,
    depth,
    wet,
    ids,
    counts,
    weights,
    consts,
    theta_out,
    surface_out,
    fp,
    ys,
    yr,
    zb,
    ex,
    tsend,
    trecv,
    table,
    wbuf,
    cbuf,
    idbuf,
    cntbuf,
    wetbuf,
    coef,
    pb,
    dbuf,
    imp,
    pcr,
    grid,
    red,
    redr,
    lsem,
    hs,
    hr,
    es,
    er,
    rs,
    rr,
):
    comp = lax.axis_index("comp")
    gx = lax.axis_index("gx")
    gy = lax.axis_index("gy")
    sources = 3 * n_gy
    units = (CX // 4) * (CY // 4)
    is_ocean = comp == 0
    is_air = comp == 1
    has_south = gy > 0
    has_north = gy < n_gy - 1

    def place(dc, dx, dy):
        return (lax.rem(comp + dc, 2), lax.rem(gx + dx + n_gx, n_gx), lax.rem(gy + dy + n_gy, n_gy))

    halo_peers = [
        place(0, 1, 0),
        place(0, -1, 0),
        place(0, 0, 1),
        place(0, 0, -1),
        place(0, 1, 1),
        place(0, -1, 1),
        place(0, 1, -1),
        place(0, -1, -1),
    ]
    export_peers = [(d, j, place(1, d, j)) for d in (-1, 0, 1) for j in range(n_gy)]
    sum_phases = []
    sum_phases.append([place(dc, 0, j) for dc in range(2) for j in range(n_gy) if dc or j])
    stride = 1
    for size in radices(n_gx):
        digit = lax.rem(gx // stride, size)
        group = []
        for j in range(1, size):
            group.append((comp, gx + (lax.rem(digit + j, size) - digit) * stride, gy))
        sum_phases.append(group)
        stride *= size

    loads = {}

    def load(name, index, src, dst):
        copy = pltpu.make_async_copy(src, dst, lsem.at[index])
        copy.start()
        loads.setdefault(name, []).append(copy)

    def loaded(name):
        for copy in loads.pop(name):
            copy.wait()

    load("export", 0, theta.at[0, 0], grid.at[0])
    load("export", 1, surface.at[0], grid.at[1])
    load("export", 2, wet, wetbuf)
    load("export", 3, kappa.at[0], grid.at[2])
    load("export", 4, depth, grid.at[3])
    for x in range(CX):
        load("theta", 8 + x, theta.at[0, :, x, :], fp.at[0, x + 1, pl.ds(0, LEV), :])
    load("remap", 5, ids.at[0], idbuf)
    load("remap", 6, counts.at[0], cntbuf)
    load("tables", 7, consts, cbuf)
    load("weights", 40, weights.at[0], wbuf)

    barrier = pltpu.get_barrier_semaphore()
    greeted = halo_peers + [p for _, _, p in export_peers] + [p for g in sum_phases for p in g]
    for peer in greeted:
        pl.semaphore_signal(barrier, inc=1, device_id=peer, device_id_type=MESH)

    lane128 = lax.broadcasted_iota(jnp.int32, (8, 128), 1)
    lane1 = lax.broadcasted_iota(jnp.int32, (1, 128), 1)

    loaded("export")
    wet_float = wetbuf[...].astype(F32)
    grid[4] = wet_float
    top = grid[0]

    ex[0] = jnp.where(is_ocean, top * wet_float, top)
    ex[1] = jnp.where(is_ocean, wet_float, grid[1])
    parts = [ex[f, pl.ds(dx, 8, stride=4), :] for f in range(2) for dx in range(4)]
    for h in range(8):
        acc = jnp.zeros((8, 128), F32)
        for j in range(8):
            shift = ((j - h) * 16) % 128
            moved = pltpu.roll(parts[j], shift, 1) if shift else parts[j]
            acc = jnp.where(lane128 // 16 == j, moved, acc)
        tsend[pl.ds(8 * h, 8), :] = acc

    for x in range(CX):
        fp[0, x + 1, SURF : SURF + 1, :] = grid[1, x : x + 1, :]
        fp[0, x + 1, SURF + 1 : SURF + 2, :] = grid[2, x : x + 1, :]
        fp[0, x + 1, SURF + 2 : SURF + 3, :] = grid[3, x : x + 1, :]
        fp[0, x + 1, SURF + 3 : SURF + 4, :] = grid[4, x : x + 1, :]
        fp[0, x + 1, SURF + 4 : SURF + 8, :] = jnp.zeros((4, 128), F32)

    def pack(s):
        def body(x, accs):
            accs = list(accs)
            for b in range(7):
                base = 2 * x + 64 * (b % 2)
                moved = pltpu.roll(fp[s, x + 1, 8 * b : 8 * b + 8, :], base + 1, 1)
                accs[b // 2] = jnp.where(
                    (lane128 == base) | (lane128 == base + 1), moved, accs[b // 2]
                )
            return tuple(accs)

        zero = jnp.zeros((8, 128), F32)
        accs = lax.fori_loop(0, CX, body, (zero,) * 4, unroll=PACK)
        for j in range(4):
            ys[s, j] = accs[j]

    def copy_to(s, d):
        if d == 0:
            src, dst, peer = fp.at[s, CX], fp.at[s, 0], halo_peers[0]
        elif d == 1:
            src, dst, peer = fp.at[s, 1], fp.at[s, CX + 1], halo_peers[1]
        else:
            src, dst, peer = ys.at[s], yr.at[s, d - 2], halo_peers[d]
        return pltpu.make_async_remote_copy(
            src_ref=src,
            dst_ref=dst,
            send_sem=hs.at[s, d],
            recv_sem=hr.at[s, d],
            device_id=peer,
            device_id_type=MESH,
        )

    def send_halo(s):
        for d in range(4):
            copy_to(s, d).start()

        @pl.when(is_air)
        def _():
            for d in range(4, 8):
                copy_to(s, d).start()

    def wait_halo(s):
        for d in range(4):
            copy_to(s, d).wait_recv()

        @pl.when(is_air)
        def _():
            for d in range(4, 8):
                copy_to(s, d).wait_recv()

    def drain_halo(s):
        for d in range(4):
            copy_to(s, d).wait_send()

        @pl.when(is_air)
        def _():
            for d in range(4, 8):
                copy_to(s, d).wait_send()

    def merged(s, south, north):
        found = []
        for j in range(4):
            low = yr[s, south, j]
            high = pltpu.roll(yr[s, north, j], 126, 1)
            found.append(jnp.where(lane128 % 2 == 0, low, high))
        return found

    def unpack(s, corners):
        own = merged(s, 0, 1)

        def fill(x, vectors, slab):
            for b in range(7):
                shift = lax.rem(256 - 2 * x - 64 * (b % 2), 128)
                zb[slab, 8 * b : 8 * b + 8, :] = pltpu.roll(vectors[b // 2], shift, 1)

        def body(x, carry):
            fill(x, own, x + 1)
            return carry

        lax.fori_loop(0, CX, body, 0, unroll=UNPACK)
        if corners:
            fill(CX - 1, merged(s, 2, 4), 0)
            fill(0, merged(s, 3, 5), CX + 1)

    def export_copy(d, j, peer):
        slot = (1 - d) * n_gy + gy
        return pltpu.make_async_remote_copy(
            src_ref=tsend,
            dst_ref=trecv.at[slot],
            send_sem=es.at[(d + 1) * n_gy + j],
            recv_sem=er.at[slot],
            device_id=peer,
            device_id_type=MESH,
        )

    loaded("theta")
    pack(0)
    pl.semaphore_wait(barrier, len(greeted))
    for d, j, peer in export_peers:
        export_copy(d, j, peer).start()
    send_halo(0)

    loaded("remap")
    loaded("tables")
    cnt = cntbuf[...].astype(F32)
    lane32 = lax.broadcasted_iota(jnp.int32, (32, 32), 1)
    row32 = lax.broadcasted_iota(jnp.int32, (32, 32), 0)
    ones = jnp.ones((32, 128), BF16)
    counted = []
    for tx in range(8):
        spread = jnp.where(lane32 == row32, jnp.broadcast_to(cnt[tx : tx + 1, :], (32, 32)), 0.0)
        counted.append(dot(spread.astype(BF16), ones)[:, :SLOTS])
    counted = jnp.concatenate(counted, axis=0)
    id_all = idbuf[...].reshape(units, SLOTS)
    slot_lane = lax.broadcasted_iota(jnp.int32, (units, SLOTS), 1)
    dev = id_all // units
    unit = id_all - dev * units
    dev_gx = dev // n_gy
    dev_gy = dev - dev_gx * n_gy
    tile_x = unit // 32
    tile_y = unit - tile_x * 32
    offset = dev_gx - gx + 1
    offset = jnp.where(offset < 0, offset + n_gx, jnp.where(offset >= n_gx, offset - n_gx, offset))
    key = (offset * n_gy + dev_gy) * 64 + (tile_y // 4) * 8 + tile_x
    key = jnp.where(slot_lane.astype(F32) < counted, key, -1)
    tile_low = tile_y - (tile_y // 4) * 4

    wait_halo(0)
    unpack(0, True)

    def rims(s, row):
        pass

    def lanes_of(shape):
        return lax.broadcasted_iota(jnp.int32, shape, 1)

    lane_full = lanes_of((CX, CY))

    def gather_row(s, row, slot):
        for x in range(CX):
            grid[slot, x : x + 1, :] = fp[s, x + 1, row : row + 1, :]

    def rim_row(row, slot):
        for x in range(CX):
            grid[slot, x : x + 1, :] = zb[x + 1, row : row + 1, :]

    def shifted(center, west_row, east_row, rim):
        row_place = lax.broadcasted_iota(jnp.int32, (CX, CY), 0)
        east = jnp.where(row_place == CX - 1, east_row, pltpu.roll(center, CX - 1, 0))
        west = jnp.where(row_place == 0, west_row, pltpu.roll(center, 1, 0))
        north = jnp.where(lane_full == CY - 1, rim, pltpu.roll(center, CY - 1, 1))
        south = jnp.where(lane_full == 0, rim, pltpu.roll(center, 1, 1))
        return east, west, north, south

    def side_rows(s, row):
        return fp[s, 0, row : row + 1, :], fp[s, CX + 1, row : row + 1, :]

    @pl.when(is_ocean)
    def _():
        wet_c = grid[4]
        rim_row(SURF + 3, 5)
        we, ww, wn, ws = shifted(wet_c, *side_rows(0, SURF + 3), grid[5])
        wn = jnp.where((lane_full == CY - 1) & jnp.logical_not(has_north), 0.0, wn)
        ws = jnp.where((lane_full == 0) & jnp.logical_not(has_south), 0.0, ws)
        for row, slot, at in ((SURF + 1, 2, 0), (SURF + 2, 3, 6)):
            center = grid[slot]
            rim_row(row, 5)
            ke, kw, kn, ks = shifted(center, *side_rows(0, row), grid[5])
            base = center * wet_c
            coef[at] = 0.5 * (base + ke * we) * wet_c * we
            coef[at + 1] = 0.5 * (kw * ww + base) * ww * wet_c
            coef[at + 2] = 0.5 * (base + kn * wn) * wet_c * wn
            coef[at + 3] = 0.5 * (ks * ws + base) * ws * wet_c
        coef[4] = (
            1.0 - (coef[0] + coef[1] + coef[2] + coef[3]) - (2.0 * vertical_mix) * wet_c
        )
        coef[5] = vertical_mix * wet_c
        diagonal = damping + coef[6] + coef[7] + coef[8] + coef[9]
        coef[10] = diagonal
        main = wet_c * diagonal + (1.0 - wet_c)
        lower = jnp.where(lane_full == 0, 0.0, -coef[9])
        upper = jnp.where(lane_full == CY - 1, 0.0, -coef[8])
        step = 1
        index = 0
        while step < CY:
            back = CY - step
            below_main = pltpu.roll(main, step, 1)
            above_main = pltpu.roll(main, back, 1)
            factor_below = -lower / below_main
            factor_above = -upper / above_main
            pcr[index] = factor_below
            pcr[index + 1] = factor_above
            main = (
                main
                + factor_below * pltpu.roll(upper, step, 1)
                + factor_above * pltpu.roll(lower, back, 1)
            )
            lower = factor_below * pltpu.roll(lower, step, 1)
            upper = factor_above * pltpu.roll(upper, back, 1)
            step *= 2
            index += 2
        pcr[14] = 1.0 / main

    def solve(values):
        step = 1
        index = 0
        while step < CY:
            values = (
                values
                + pcr[index] * pltpu.roll(values, step, 1)
                + pcr[index + 1] * pltpu.roll(values, CY - step, 1)
            )
            step *= 2
            index += 2
        return values * pcr[14]

    lane56 = lanes_of((ROWS, CY))
    row56 = lax.broadcasted_iota(jnp.int32, (ROWS, CY), 0)
    row48 = lax.broadcasted_iota(jnp.int32, (LEV, CY), 0)
    lane48 = lanes_of((LEV, CY))

    def ocean_step(s):
        def body(x, carry):
            c = fp[s - 1, x + 1, 0:LEV, :]
            w = fp[s - 1, x, 0:LEV, :]
            e = fp[s - 1, x + 2, 0:LEV, :]
            z = zb[x + 1, 0:LEV, :]

            def row(i):
                return coef[i, pl.ds(x, 1), :]

            n = jnp.where(lane48 == CY - 1, z, pltpu.roll(c, CY - 1, 1))
            o = jnp.where(lane48 == 0, z, pltpu.roll(c, 1, 1))
            up = jnp.where(row48 == LEV - 1, c, pltpu.roll(c, LEV - 1, 0))
            down = jnp.where(row48 == 0, c, pltpu.roll(c, 1, 0))
            new = (
                row(4) * c
                + row(0) * e
                + row(1) * w
                + row(2) * n
                + row(3) * o
                + row(5) * (up + down)
            )
            fp[s, x + 1, 0:LEV, :] = new
            if s > 1:
                fp[s, x + 1, 0:1, :] = new[0:1, :] + grid[7, pl.ds(x, 1), :]
            return carry

        lax.fori_loop(0, CX, body, 0, unroll=OCEAN)

    def air_step(s):
        h = jnp.where(
            ((lane1 % 4 == 0) & ((lane1 > 0) | has_south))
            | ((lane1 % 4 == 3) & ((lane1 < CY - 1) | has_north)),
            0.5,
            0.0,
        )
        mix_up = jnp.where(row56 < LEV - 1, vertical_mix, 0.0)
        mix_down = jnp.where((row56 > 0) & (row56 < LEV), vertical_mix, 0.0)

        def body(i, carry):
            x0 = 4 * i
            v = [fp[s - 1, x0 + j] for j in range(6)]
            z = [zb[x0 + j] for j in range(6)]

            def across(t):
                return [0.5 * (t[1] + t[0]), t[2], t[3], 0.5 * (t[4] + t[5])]

            blocks = []
            for a, za in zip(across(v), across(z)):
                partner = jnp.where(lane56 % 4 == 0, pltpu.roll(a, 1, 1), pltpu.roll(a, CY - 1, 1))
                partner = jnp.where((lane56 == 0) | (lane56 == CY - 1), za, partner)
                blocks.append(a + h * (partner - a))
            high, low = split(jnp.concatenate(blocks, axis=0))
            along = dot(jnp.concatenate([high, low], axis=1), cbuf[256:512, :])
            along = along[:, :CY] + along[:, CY:]
            for j in range(4):
                b = blocks[j]
                lap = along[ROWS * j : ROWS * (j + 1)]
                for m in range(4):
                    lap = lap + float(second_derivative[j, m]) * blocks[m]
                up = pltpu.roll(b, ROWS - 1, 0)
                down = pltpu.roll(b, 1, 0)
                new = (
                    b
                    + grid[2, pl.ds(x0 + j, 1), :] * lap
                    + mix_up * (up - b)
                    + mix_down * (down - b)
                )
                x = x0 + j
                fp[s, x + 1] = new
                if s == 1:
                    grid[8, pl.ds(x, 1), :] = b[0:1, :]
                    grid[9, pl.ds(x, 1), :] = b[SURF : SURF + 1, :]
                else:
                    fp[s, x + 1, 0:1, :] = (
                        new[0:1, :]
                        + grid[6, pl.ds(x, 1), :]
                        - grid[7, pl.ds(x, 1), :] * b[0:1, :]
                    )
                    if s <= ITERS:
                        fp[s, x + 1, SURF : SURF + 1, :] = (
                            new[SURF : SURF + 1, :]
                            + grid[10, pl.ds(x, 1), :]
                            - press_rate * b[SURF : SURF + 1, :]
                        )
            return carry

        lax.fori_loop(0, CX // 4, body, 0, unroll=AIR)

    def forward(s):
        @pl.when(is_ocean)
        def _():
            ocean_step(s)

        @pl.when(is_air)
        def _():
            air_step(s)

    forward(1)

    for d in range(3):
        for j in range(n_gy):
            slot = d * n_gy + j
            pltpu.make_async_remote_copy(
                src_ref=tsend,
                dst_ref=trecv.at[slot],
                send_sem=es.at[slot],
                recv_sem=er.at[slot],
                device_id=halo_peers[0],
                device_id_type=MESH,
            ).wait_recv()
    high, low = split(trecv[...].reshape(sources * 64, 128))
    table[:, 0:128] = high
    table[:, 128:256] = low
    key_lane = lax.broadcasted_iota(jnp.int32, (units, sources * 64), 1)
    lane256 = lax.broadcasted_iota(jnp.int32, (units, 256), 1)
    low_lane = (lane256 // 4) % 4
    slot_of = (lane256 // 16) % 8
    picked = jnp.zeros((units, 256), F32)
    for m in range(SLOTS):
        hot = jnp.where(key[:, m : m + 1] == key_lane, 1.0, 0.0).astype(BF16)
        found = dot(hot, table[...])
        found = jnp.where(low_lane == tile_low[:, m : m + 1], found, 0.0).astype(BF16)
        picked = jnp.where(slot_of == m, dot(found, cbuf[0:256, :]), picked)
    high, low = split(picked)
    pb[0] = high[:, 0:128]
    pb[1] = high[:, 128:256]
    pb[2] = low[:, 0:128]
    pb[3] = low[:, 128:256]
    loaded("weights")
    own_tile = lax.broadcasted_iota(jnp.int32, (16, 256), 0) == (
        lax.broadcasted_iota(jnp.int32, (16, 256), 1) // 16
    )
    for g in range(16):
        left = pb[:, 16 * g : 16 * g + 16, :].reshape(64, 128)
        right = wbuf[g // 2, 16 * (g % 2) : 16 * (g % 2) + 16].reshape(256, 128)
        out = lax.dot_general(
            left, right, (((1,), (1,)), ((), ())), preferred_element_type=F32
        )
        for f in range(2):
            value = out[16 * f : 16 * f + 16] + out[32 + 16 * f : 48 + 16 * f]
            value = jnp.sum(jnp.where(own_tile, value, 0.0), axis=0, keepdims=True)
            for u in range(2):
                dbuf[f, 2 * (g % 2) + u, g // 2 : g // 2 + 1, :] = value[:, 128 * u : 128 * u + 128]
    high, low = split(dbuf[...].reshape(64, 128))
    turned = dot(jnp.concatenate([high, low], axis=0), cbuf[512:640, 0:128])
    turned = turned[:64] + turned[64:]
    for f in range(2):
        quarters = [turned[32 * f + 8 * q : 32 * f + 8 * q + 8] for q in range(4)]
        for dx in range(4):
            acc = jnp.zeros((8, 128), F32)
            for q in range(4):
                shift = ((q - dx) * 32) % 128
                moved = pltpu.roll(quarters[q], shift, 1) if shift else quarters[q]
                acc = jnp.where(lane128 // 32 == q, moved, acc)
            imp[f, pl.ds(dx, 8, stride=4), :] = acc

    wet_c = grid[4]
    heat = jnp.where(is_ocean, -(wet_c * imp[0]), grid[0])
    cells = jnp.where(is_ocean, wet_c, 0.0)
    row8 = lax.broadcasted_iota(jnp.int32, (8, 128), 0)

    def rows8(v):
        return jnp.sum(v, axis=0, keepdims=True)

    red[0] = jnp.where(row8 == 0, rows8(heat), jnp.where(row8 == 1, rows8(cells), 0.0))

    def sum_copy(phase, j):
        return pltpu.make_async_remote_copy(
            src_ref=red.at[phase],
            dst_ref=redr.at[phase, j],
            send_sem=rs.at[phase, j],
            recv_sem=rr.at[phase, j],
            device_id=sum_phases[phase][j],
            device_id_type=MESH,
        )

    def sum_send(phase):
        for j in range(len(sum_phases[phase])):
            sum_copy(phase, j).start()

    def sum_finish(phase):
        total = red[phase]
        for j in range(len(sum_phases[phase])):
            sum_copy(phase, j).wait_recv()
            total = total + redr[phase, j]
        red[phase + 1] = total

    sum_send(0)

    centre = (bound_high + bound_low) / 2.0
    half_range = (bound_high - bound_low) / 2.0
    spread_ratio = centre / half_range

    def apply_a(s, center):
        rim_row(SURF, 5)
        east, west, north, south = shifted(center, *side_rows(s, SURF), grid[5])
        near = coef[6] * east + coef[7] * west + coef[8] * north + coef[9] * south
        return wet_c * (coef[10] * center - near) + (1.0 - wet_c) * center

    def put_surface(s, value):
        grid[13] = value
        for x in range(CX):
            fp[s, x + 1, SURF : SURF + 1, :] = grid[13, x : x + 1, :]

    @pl.when(is_ocean)
    def _():
        force = heat_rate * wet_c * imp[0]
        grid[7] = force
        for x in range(CX):
            fp[1, x + 1, 0:1, :] = fp[1, x + 1, 0:1, :] + grid[7, x : x + 1, :]
        eta = grid[1]
        residual = wet_c * (damping * eta + fresh_rate * imp[1]) - apply_a(0, eta)
        direction = solve(residual) / centre
        grid[11] = eta + direction
        grid[12] = residual
        put_surface(1, direction)

    @pl.when(is_air)
    def _():
        grid[6] = air_rate * imp[0]
        grid[7] = air_rate * imp[1]
        grid[10] = press_rate * imp[0]
        grid[5] = grid[6] - grid[7] * grid[8]
        grid[11] = grid[10] - press_rate * grid[9]
        for x in range(CX):
            fp[1, x + 1, 0:1, :] = fp[1, x + 1, 0:1, :] + grid[5, x : x + 1, :]
            fp[1, x + 1, SURF : SURF + 1, :] = (
                fp[1, x + 1, SURF : SURF + 1, :] + grid[11, x : x + 1, :]
            )

    recurrence = 1.0 / spread_ratio
    phases = len(sum_phases)
    for s in range(2, NSTEP + 1):
        pack(s - 1)
        send_halo(s - 1)
        if s - 2 >= 1 and s - 2 < phases:
            sum_send(s - 2)
        wait_halo(s - 1)
        unpack(s - 1, True)
        forward(s)
        if s - 2 < phases:
            sum_finish(s - 2)
        if s <= ITERS:
            recurrence_next = 1.0 / (2.0 * spread_ratio - recurrence)

            @pl.when(is_ocean)
            def _(s=s, recurrence=recurrence, recurrence_next=recurrence_next):
                old = grid[13]
                residual = grid[12] - apply_a(s - 1, old)
                direction = (recurrence_next * recurrence) * old + (
                    2.0 * recurrence_next / half_range
                ) * solve(residual)
                grid[11] = grid[11] + direction
                grid[12] = residual
                put_surface(s, direction)

            recurrence = recurrence_next
        if s == ITERS:

            @pl.when(is_air)
            def _(s=s):
                gather_row(s, SURF, 11)

            loads["surface"] = [pltpu.make_async_copy(grid.at[11], surface_out.at[0], lsem.at[41])]
            loads["surface"][0].start()

    total = red[phases]
    correction = jnp.sum(total[0:1, :], axis=1, keepdims=True) / jnp.sum(
        total[1:2, :], axis=1, keepdims=True
    )
    response = heat_response()

    @pl.when(is_ocean)
    def _():
        spread = jnp.zeros((8, 128), F32)
        for k in range(NSTEP):
            spread = jnp.where(row8 == k, response[k], spread)
        spread = spread * correction

        def body(x, carry):
            fp[NSTEP, x + 1, 0:8, :] = (
                fp[NSTEP, x + 1, 0:8, :] + spread * grid[4, pl.ds(x, 1), :]
            )
            return carry

        lax.fori_loop(0, CX, body, 0)

    stores = []
    for x in range(CX):
        copy = pltpu.make_async_copy(
            fp.at[NSTEP, x + 1, pl.ds(0, LEV), :], theta_out.at[0, :, x, :], lsem.at[8 + x]
        )
        copy.start()
        stores.append(copy)
    for s in range(NSTEP):
        drain_halo(s)
    for d, j, peer in export_peers:
        export_copy(d, j, peer).wait_send()
    for phase in range(phases):
        for j in range(len(sum_phases[phase])):
            sum_copy(phase, j).wait_send()
    loaded("surface")
    for copy in stores:
        copy.wait()


def solution(mesh):
    n_gx = mesh.shape["gx"]
    n_gy = mesh.shape["gy"]
    sources = 3 * n_gy
    phases = 1 + len(radices(n_gx))
    widest = max(2 * n_gy - 1, 3)
    constants = tables()

    def per_device(theta, surface, kappa, depth, wet, ids, counts, weights):
        spec = pl.BlockSpec(memory_space=pl.ANY)
        dma = pltpu.SemaphoreType.DMA
        return pl.pallas_call(
            functools.partial(kernel, n_gx, n_gy),
            out_shape=(
                jax.ShapeDtypeStruct((1, LEV, CX, CY), F32),
                jax.ShapeDtypeStruct((1, CX, CY), F32),
            ),
            in_specs=[spec] * 9,
            out_specs=(spec, spec),
            scratch_shapes=[
                pltpu.VMEM((NSTEP + 1, CX + 2, ROWS, CY), F32),
                pltpu.VMEM((NSTEP, 4, 8, CY), F32),
                pltpu.VMEM((NSTEP, 6, 4, 8, CY), F32),
                pltpu.VMEM((CX + 2, ROWS, CY), F32),
                pltpu.VMEM((2, CX, CY), F32),
                pltpu.VMEM((64, 128), F32),
                pltpu.VMEM((sources, 64, 128), F32),
                pltpu.VMEM((sources * 64, 256), BF16),
                pltpu.VMEM((8, 32, 16, 128), BF16),
                pltpu.VMEM((640, 256), BF16),
                pltpu.VMEM((8, 32, SLOTS), jnp.int32),
                pltpu.VMEM((8, 32), jnp.int32),
                pltpu.VMEM((CX, CY), jnp.int32),
                pltpu.VMEM((11, CX, CY), F32),
                pltpu.VMEM((4, 256, 128), BF16),
                pltpu.VMEM((2, 4, 8, 128), F32),
                pltpu.VMEM((2, CX, CY), F32),
                pltpu.VMEM((15, CX, CY), F32),
                pltpu.VMEM((14, CX, CY), F32),
                pltpu.VMEM((phases + 1, 8, 128), F32),
                pltpu.VMEM((phases, widest, 8, 128), F32),
                dma((42,)),
                dma((NSTEP, 8)),
                dma((NSTEP, 8)),
                dma((sources,)),
                dma((sources,)),
                dma((phases, widest)),
                dma((phases, widest)),
            ],
            compiler_params=pltpu.CompilerParams(
                collective_id=0, has_side_effects=True, vmem_limit_bytes=60 * 1024 * 1024
            ),
        )(theta, surface, kappa, depth, wet, ids, counts, weights, jnp.asarray(constants))

    in_specs = (
        P("comp", None, "gx", "gy"),
        P("comp", "gx", "gy"),
        P("comp", "gx", "gy"),
        P("gx", "gy"),
        P("gx", "gy"),
        P("comp", "gx", "gy", None),
        P("comp", "gx", "gy"),
        P("comp", "gx", "gy", None, None),
    )
    out_specs = (P("comp", None, "gx", "gy"), P("comp", "gx", "gy"))
    return jax.shard_map(
        per_device, mesh=mesh, in_specs=in_specs, out_specs=out_specs, check_vma=False
    )
```

```python
import functools

import jax
import jax.numpy as jnp
import ml_dtypes
import numpy as np
from jax import lax
from jax.experimental import pallas as pl
from jax.experimental.pallas import tpu as pltpu
from jax.sharding import PartitionSpec as P

MESH = pl.DeviceIdType.MESH
F32 = jnp.float32
BF16 = jnp.bfloat16

NSTEP = 6
ITERS = 4
SLOTS = 8
LEV = 48
CX = 32
CY = 128
ROWS = 56
SURF = 48
EDGE = (0, 1, 2, 3, 28, 29, 30, 31)
INNER = tuple(range(4, 28))

node_derivative = np.array(
    [
        [-3.0, 4.045084971874737, -1.545084971874737, 0.5],
        [-0.809016994374947, 0.0, 1.118033988749895, -0.309016994374947],
        [0.309016994374947, -1.118033988749895, 0.0, 0.809016994374947],
        [-0.5, 1.545084971874737, -4.045084971874737, 3.0],
    ]
)
second_derivative = node_derivative @ node_derivative
vertical_mix = 0.2
heat_rate = 0.5
air_rate = 0.3
press_rate = 0.1
damping = 0.05
fresh_rate = 0.5
bound_low = 0.02
bound_high = 2.0


def heat_response():
    level = np.zeros(LEV)
    for _ in range(NSTEP):
        change = level[1:] - level[:-1]
        level = level + vertical_mix * (np.append(change, 0.0) - np.append(0.0, change))
        level[0] += heat_rate
    return [float(v) for v in level]


def halves(table):
    high = table.astype(ml_dtypes.bfloat16)
    low = (table - high.astype(np.float64)).astype(ml_dtypes.bfloat16)
    return high, low


def tables():
    lane = np.arange(256)
    f_in, dx_in, dy_in = (lane // 64) % 2, (lane // 16) % 4, lane % 4
    f_out, dx_out, dy_out = lane // 128, (lane // 4) % 4, lane % 4
    fold = (
        (f_in[:, None] == f_out[None])
        & (dx_in[:, None] == dx_out[None])
        & (dy_in[:, None] == dy_out[None])
    )
    block = np.kron(np.eye(32), second_derivative.T)
    high, low = halves(block)
    zero = np.zeros((128, 128))
    lap = np.block(
        [[high.astype(np.float64), low.astype(np.float64)], [high.astype(np.float64), zero]]
    )
    lane = np.arange(128)
    target = ((lane // 4) % 4) * 32 + (lane // 16) * 4 + lane % 4
    perm = np.zeros((128, 256))
    perm[lane, target] = 1.0
    return np.concatenate([fold.astype(np.float64), lap, perm]).astype(ml_dtypes.bfloat16)


def split(value):
    high = value.astype(BF16)
    low = (value - high.astype(F32)).astype(BF16)
    return high, low


def dot(a, b):
    return jnp.dot(a, b, preferred_element_type=F32)


def radices(count):
    if count == 32:
        return [4, 2, 4]
    found = []
    while count > 1:
        size = 4 if count % 4 == 0 else count
        found.append(size)
        count //= size
    return found


def kernel(
    n_gx,
    n_gy,
    theta,
    surface,
    kappa,
    depth,
    wet,
    ids,
    counts,
    weights,
    consts,
    theta_out,
    surface_out,
    fp,
    ys,
    yr,
    ye,
    yer,
    zb,
    ex,
    tsend,
    trecv,
    table,
    wbuf,
    cbuf,
    idbuf,
    cntbuf,
    wetbuf,
    coef,
    pb,
    dbuf,
    imp,
    pcr,
    grid,
    red,
    redr,
    lsem,
    hs,
    hr,
    es,
    er,
    rs,
    rr,
):
    comp = lax.axis_index("comp")
    gx = lax.axis_index("gx")
    gy = lax.axis_index("gy")
    sources = 3 * n_gy
    units = (CX // 4) * (CY // 4)
    is_ocean = comp == 0
    is_air = comp == 1
    has_south = gy > 0
    has_north = gy < n_gy - 1

    def place(dc, dx, dy):
        return (lax.rem(comp + dc, 2), lax.rem(gx + dx + n_gx, n_gx), lax.rem(gy + dy + n_gy, n_gy))

    halo_peers = [
        place(0, 1, 0),
        place(0, -1, 0),
        place(0, 0, 1),
        place(0, 0, -1),
        place(0, 1, 1),
        place(0, -1, 1),
        place(0, 1, -1),
        place(0, -1, -1),
    ]
    export_peers = [(d, j, place(1, d, j)) for d in (-1, 0, 1) for j in range(n_gy)]
    sum_phases = []
    sum_phases.append([place(dc, 0, j) for dc in range(2) for j in range(n_gy) if dc or j])
    stride = 1
    for size in radices(n_gx):
        digit = lax.rem(gx // stride, size)
        group = []
        for j in range(1, size):
            group.append((comp, gx + (lax.rem(digit + j, size) - digit) * stride, gy))
        sum_phases.append(group)
        stride *= size

    loads = {}

    def load(name, index, src, dst):
        copy = pltpu.make_async_copy(src, dst, lsem.at[index])
        copy.start()
        loads.setdefault(name, []).append(copy)

    def loaded(name):
        for copy in loads.pop(name):
            copy.wait()

    load("export", 0, theta.at[0, 0], grid.at[0])
    load("export", 1, surface.at[0], grid.at[1])
    load("export", 2, wet, wetbuf)
    load("export", 3, kappa.at[0], grid.at[2])
    load("export", 4, depth, grid.at[3])
    for x in range(CX):
        load("theta", 8 + x, theta.at[0, :, x, :], fp.at[0, x + 1, pl.ds(0, LEV), :])
    load("remap", 5, ids.at[0], idbuf)
    load("remap", 6, counts.at[0], cntbuf)
    load("tables", 7, consts, cbuf)
    load("weights", 40, weights.at[0], wbuf)

    barrier = pltpu.get_barrier_semaphore()
    greeted = halo_peers + [p for _, _, p in export_peers] + [p for g in sum_phases for p in g]
    for peer in greeted:
        pl.semaphore_signal(barrier, inc=1, device_id=peer, device_id_type=MESH)

    lane128 = lax.broadcasted_iota(jnp.int32, (8, 128), 1)
    lane1 = lax.broadcasted_iota(jnp.int32, (1, 128), 1)

    loaded("export")
    wet_float = wetbuf[...].astype(F32)
    grid[4] = wet_float
    top = grid[0]

    ex[0] = jnp.where(is_ocean, top * wet_float, top)
    ex[1] = jnp.where(is_ocean, wet_float, grid[1])
    parts = [ex[f, pl.ds(dx, 8, stride=4), :] for f in range(2) for dx in range(4)]
    for h in range(8):
        acc = jnp.zeros((8, 128), F32)
        for j in range(8):
            shift = ((j - h) * 16) % 128
            moved = pltpu.roll(parts[j], shift, 1) if shift else parts[j]
            acc = jnp.where(lane128 // 16 == j, moved, acc)
        tsend[pl.ds(8 * h, 8), :] = acc

    for x in range(CX):
        fp[0, x + 1, SURF : SURF + 1, :] = grid[1, x : x + 1, :]
        fp[0, x + 1, SURF + 1 : SURF + 2, :] = grid[2, x : x + 1, :]
        fp[0, x + 1, SURF + 2 : SURF + 3, :] = grid[3, x : x + 1, :]
        fp[0, x + 1, SURF + 3 : SURF + 4, :] = grid[4, x : x + 1, :]
        fp[0, x + 1, SURF + 4 : SURF + 8, :] = jnp.zeros((4, 128), F32)

    def place_in(acc, moved, lane):
        return jnp.where((lane128 == lane) | (lane128 == lane + 1), moved, acc)

    def pack_inner(s, slabs, blocks):
        for j in range(4):
            acc = jnp.zeros((8, 128), F32)
            found = False
            for b in (2 * j, 2 * j + 1):
                if b in blocks:
                    found = True
                    for x in slabs:
                        lane = 2 * x + 64 * (b % 2)
                        moved = pltpu.roll(fp[s, x + 1, 8 * b : 8 * b + 8, :], (lane + 1) % 128, 1)
                        acc = place_in(acc, moved, lane)
            if found:
                ys[s, j] = acc

    def pack_edge(s, blocks):
        acc = jnp.zeros((8, 128), F32)
        for b in blocks:
            for e, x in enumerate(EDGE):
                lane = 16 * b + 2 * e
                moved = pltpu.roll(fp[s, x + 1, 8 * b : 8 * b + 8, :], lane + 1, 1)
                acc = place_in(acc, moved, lane)
        ye[s] = acc

    def merge(low, high):
        return jnp.where(lane128 % 2 == 0, low, pltpu.roll(high, 126, 1))

    def turn(value, lane):
        return pltpu.roll(value, (128 - lane) % 128, 1) if lane % 128 else value

    def unpack_inner(s, slabs, blocks):
        for j in range(4):
            if 2 * j in blocks or 2 * j + 1 in blocks:
                both = merge(yr[s, 0, j], yr[s, 1, j])
                for b in (2 * j, 2 * j + 1):
                    if b in blocks:
                        for x in slabs:
                            zb[x + 1, 8 * b : 8 * b + 8, :] = turn(both, 2 * x + 64 * (b % 2))

    def unpack_edge(s, blocks):
        both = merge(yer[s, 0], yer[s, 1])
        for b in blocks:
            for e, x in enumerate(EDGE):
                zb[x + 1, 8 * b : 8 * b + 8, :] = turn(both, 16 * b + 2 * e)

    def unpack_corner(s, blocks):
        west = merge(yer[s, 2], yer[s, 4])
        east = merge(yer[s, 3], yer[s, 5])
        for b in blocks:
            zb[0, 8 * b : 8 * b + 8, :] = turn(west, 16 * b + 14)
            zb[CX + 1, 8 * b : 8 * b + 8, :] = turn(east, 16 * b)

    def copy_to(s, d):
        peer = halo_peers[d % 2 if d < 4 else 2 + d % 2 if d < 10 else d - 6]
        if d < 4:
            rows = pl.ds(0, LEV) if d < 2 else pl.ds(SURF, 8)
            src = fp.at[s, CX if d % 2 == 0 else 1, rows, :]
            dst = fp.at[s, 0 if d % 2 == 0 else CX + 1, rows, :]
        elif d < 6:
            src, dst = ye.at[s], yer.at[s, d - 4]
        elif d < 8:
            src, dst = ys.at[s, pl.ds(0, 3)], yr.at[s, d - 6, pl.ds(0, 3)]
        elif d < 10:
            src, dst = ys.at[s, 3], yr.at[s, d - 8, 3]
        else:
            src, dst = ye.at[s], yer.at[s, d - 8]
        return pltpu.make_async_remote_copy(
            src_ref=src,
            dst_ref=dst,
            send_sem=hs.at[s, d],
            recv_sem=hr.at[s, d],
            device_id=peer,
            device_id_type=MESH,
        )

    SLAB, SLAB_SURF, OUTER, INSIDE, SURF_COLUMN = (0, 1), (2, 3), (4, 5), (6, 7), (8, 9)
    CORNER = (10, 11, 12, 13)

    def send(s, *kinds):
        for kind in kinds:
            for d in kind:
                copy_to(s, d).start()

    def wait(s, *kinds):
        for kind in kinds:
            for d in kind:
                copy_to(s, d).wait_recv()

    def drain_halo(s):
        kinds = [SLAB, OUTER, INSIDE]
        if s < ITERS:
            kinds += [SLAB_SURF, SURF_COLUMN]
        for kind in kinds:
            for d in kind:
                copy_to(s, d).wait_send()

        @pl.when(is_air)
        def _():
            for d in CORNER:
                copy_to(s, d).wait_send()

    def export_copy(d, j, peer):
        slot = (1 - d) * n_gy + gy
        return pltpu.make_async_remote_copy(
            src_ref=tsend,
            dst_ref=trecv.at[slot],
            send_sem=es.at[(d + 1) * n_gy + j],
            recv_sem=er.at[slot],
            device_id=peer,
            device_id_type=MESH,
        )

    ALL = tuple(range(CX))
    LEVELS = tuple(range(6))
    BOTH = tuple(range(7))
    pl.semaphore_wait(barrier, len(greeted))
    for d, j, peer in export_peers:
        export_copy(d, j, peer).start()
    loaded("theta")
    send(0, SLAB, SLAB_SURF)
    pack_edge(0, BOTH)
    send(0, OUTER)

    @pl.when(is_air)
    def _():
        send(0, CORNER)

    pack_inner(0, INNER, LEVELS)
    pack_inner(0, ALL, (6,))
    send(0, INSIDE, SURF_COLUMN)

    loaded("remap")
    loaded("tables")
    gy_bits = n_gy.bit_length() - 1
    id_all = idbuf[...]
    unit = id_all & (units - 1)
    dev = id_all >> 8
    dev_gy = dev & (n_gy - 1)
    offset = (dev >> gy_bits) - gx + 1
    offset = jnp.where(offset < 0, offset + n_gx, jnp.where(offset >= n_gx, offset - n_gx, offset))
    tile_y = unit & 31
    source = offset * n_gy + dev_gy
    row = (tile_y >> 2) * 8 + (unit >> 5)
    low_tile = tile_y & 3
    slot_order = lax.broadcasted_iota(jnp.int32, (8, SLOTS, 32), 1)
    source = jnp.where(slot_order < cntbuf[...][:, None, :], source, 200)
    eye = jnp.where(
        lax.broadcasted_iota(jnp.int32, (32, 32), 0) == lax.broadcasted_iota(jnp.int32, (32, 32), 1),
        1.0,
        0.0,
    ).astype(BF16)
    columns = []
    for tx in range(8):
        stacked = jnp.concatenate([source[tx], row[tx], low_tile[tx], low_tile[tx]], axis=0)
        columns.append(
            lax.dot_general(
                eye,
                stacked.astype(F32).astype(BF16),
                (((1,), (1,)), ((), ())),
                preferred_element_type=F32,
            )
        )
    columns = jnp.concatenate(columns, axis=0)
    key = columns[:, 0:8] * 64.0 + columns[:, 8:16]
    tile_low = columns[:, 16:24]

    wait(0, INSIDE, OUTER, SURF_COLUMN)
    unpack_inner(0, INNER, LEVELS)
    unpack_inner(0, ALL, (6,))
    unpack_edge(0, LEVELS)
    wait(0, SLAB, SLAB_SURF)

    @pl.when(is_air)
    def _():
        wait(0, CORNER)
        unpack_corner(0, BOTH)


    def lanes_of(shape):
        return lax.broadcasted_iota(jnp.int32, shape, 1)

    lane_full = lanes_of((CX, CY))

    def gather_row(s, row, slot):
        for x in range(CX):
            grid[slot, x : x + 1, :] = fp[s, x + 1, row : row + 1, :]

    def rim_row(row, slot):
        for x in range(CX):
            grid[slot, x : x + 1, :] = zb[x + 1, row : row + 1, :]

    def shifted(center, west_row, east_row, rim):
        row_place = lax.broadcasted_iota(jnp.int32, (CX, CY), 0)
        east = jnp.where(row_place == CX - 1, east_row, pltpu.roll(center, CX - 1, 0))
        west = jnp.where(row_place == 0, west_row, pltpu.roll(center, 1, 0))
        north = jnp.where(lane_full == CY - 1, rim, pltpu.roll(center, CY - 1, 1))
        south = jnp.where(lane_full == 0, rim, pltpu.roll(center, 1, 1))
        return east, west, north, south

    def side_rows(s, row):
        return fp[s, 0, row : row + 1, :], fp[s, CX + 1, row : row + 1, :]

    @pl.when(is_ocean)
    def _():
        wet_c = grid[4]
        rim_row(SURF + 3, 5)
        we, ww, wn, ws = shifted(wet_c, *side_rows(0, SURF + 3), grid[5])
        wn = jnp.where((lane_full == CY - 1) & jnp.logical_not(has_north), 0.0, wn)
        ws = jnp.where((lane_full == 0) & jnp.logical_not(has_south), 0.0, ws)
        for row, slot, at in ((SURF + 1, 2, 0), (SURF + 2, 3, 6)):
            center = grid[slot]
            rim_row(row, 5)
            ke, kw, kn, ks = shifted(center, *side_rows(0, row), grid[5])
            base = center * wet_c
            coef[at] = 0.5 * (base + ke * we) * wet_c * we
            coef[at + 1] = 0.5 * (kw * ww + base) * ww * wet_c
            coef[at + 2] = 0.5 * (base + kn * wn) * wet_c * wn
            coef[at + 3] = 0.5 * (ks * ws + base) * ws * wet_c
        coef[4] = (
            1.0 - (coef[0] + coef[1] + coef[2] + coef[3]) - (2.0 * vertical_mix) * wet_c
        )
        coef[5] = vertical_mix * wet_c
        diagonal = damping + coef[6] + coef[7] + coef[8] + coef[9]
        coef[10] = diagonal
        main = wet_c * diagonal + (1.0 - wet_c)
        lower = jnp.where(lane_full == 0, 0.0, -coef[9])
        upper = jnp.where(lane_full == CY - 1, 0.0, -coef[8])
        step = 1
        index = 0
        while step < CY:
            back = CY - step
            below_main = pltpu.roll(main, step, 1)
            above_main = pltpu.roll(main, back, 1)
            factor_below = -lower / below_main
            factor_above = -upper / above_main
            pcr[index] = factor_below
            pcr[index + 1] = factor_above
            main = (
                main
                + factor_below * pltpu.roll(upper, step, 1)
                + factor_above * pltpu.roll(lower, back, 1)
            )
            lower = factor_below * pltpu.roll(lower, step, 1)
            upper = factor_above * pltpu.roll(upper, back, 1)
            step *= 2
            index += 2
        pcr[14] = 1.0 / main

    def solve(values):
        step = 1
        index = 0
        while step < CY:
            values = (
                values
                + pcr[index] * pltpu.roll(values, step, 1)
                + pcr[index + 1] * pltpu.roll(values, CY - step, 1)
            )
            step *= 2
            index += 2
        return values * pcr[14]

    row48 = lax.broadcasted_iota(jnp.int32, (LEV, CY), 0)
    lane48 = lanes_of((LEV, CY))

    def ocean_step(s, slabs):
        for x in slabs:
            c = fp[s - 1, x + 1, 0:LEV, :]
            w = fp[s - 1, x, 0:LEV, :]
            e = fp[s - 1, x + 2, 0:LEV, :]
            z = zb[x + 1, 0:LEV, :]

            def row(i, x=x):
                return coef[i, x : x + 1, :]

            n = jnp.where(lane48 == CY - 1, z, pltpu.roll(c, CY - 1, 1))
            o = jnp.where(lane48 == 0, z, pltpu.roll(c, 1, 1))
            up = jnp.where(row48 == LEV - 1, c, pltpu.roll(c, LEV - 1, 0))
            down = jnp.where(row48 == 0, c, pltpu.roll(c, 1, 0))
            new = (
                row(4) * c
                + row(0) * e
                + row(1) * w
                + row(2) * n
                + row(3) * o
                + row(5) * (up + down)
            )
            fp[s, x + 1, 0:LEV, :] = new
            if s > 1:
                fp[s, x + 1, 0:1, :] = new[0:1, :] + grid[7, x : x + 1, :]

    def air_step(s, tiles):
        rows = ROWS if s <= ITERS else LEV
        lane_r = lanes_of((rows, CY))
        row_r = lax.broadcasted_iota(jnp.int32, (rows, CY), 0)
        h = jnp.where(
            ((lane1 % 4 == 0) & ((lane1 > 0) | has_south))
            | ((lane1 % 4 == 3) & ((lane1 < CY - 1) | has_north)),
            0.5,
            0.0,
        )
        mix_up = jnp.where(row_r < LEV - 1, vertical_mix, 0.0)
        mix_down = jnp.where((row_r > 0) & (row_r < LEV), vertical_mix, 0.0)

        for i in tiles:
            x0 = 4 * i
            v = [fp[s - 1, x0 + j, 0:rows, :] for j in range(6)]
            z = [zb[x0 + j, 0:rows, :] for j in range(6)]

            def across(t):
                return [0.5 * (t[1] + t[0]), t[2], t[3], 0.5 * (t[4] + t[5])]

            blocks = []
            for a, za in zip(across(v), across(z)):
                partner = jnp.where(lane_r % 4 == 0, pltpu.roll(a, 1, 1), pltpu.roll(a, CY - 1, 1))
                partner = jnp.where((lane_r == 0) | (lane_r == CY - 1), za, partner)
                blocks.append(a + h * (partner - a))
            high, low = split(jnp.concatenate(blocks, axis=0))
            along = dot(jnp.concatenate([high, low], axis=1), cbuf[256:512, :])
            along = along[:, :CY] + along[:, CY:]
            for j in range(4):
                b = blocks[j]
                lap = along[rows * j : rows * (j + 1)]
                for m in range(4):
                    lap = lap + float(second_derivative[j, m]) * blocks[m]
                up = pltpu.roll(b, rows - 1, 0)
                down = pltpu.roll(b, 1, 0)
                new = (
                    b
                    + grid[2, x0 + j : x0 + j + 1, :] * lap
                    + mix_up * (up - b)
                    + mix_down * (down - b)
                )
                x = x0 + j
                fp[s, x + 1, 0:rows, :] = new
                if s == 1:
                    grid[8, x : x + 1, :] = b[0:1, :]
                    grid[9, x : x + 1, :] = b[SURF : SURF + 1, :]
                else:
                    fp[s, x + 1, 0:1, :] = (
                        new[0:1, :]
                        + grid[6, x : x + 1, :]
                        - grid[7, x : x + 1, :] * b[0:1, :]
                    )
                    if s <= ITERS:
                        fp[s, x + 1, SURF : SURF + 1, :] = (
                            new[SURF : SURF + 1, :]
                            + grid[10, x : x + 1, :]
                            - press_rate * b[SURF : SURF + 1, :]
                        )


    @pl.when(is_ocean)
    def _():
        ocean_step(1, ALL)

    @pl.when(is_air)
    def _():
        unpack_edge(0, (6,))
        air_step(1, tuple(range(CX // 4)))

    for d in range(3):
        for j in range(n_gy):
            slot = d * n_gy + j
            pltpu.make_async_remote_copy(
                src_ref=tsend,
                dst_ref=trecv.at[slot],
                send_sem=es.at[slot],
                recv_sem=er.at[slot],
                device_id=halo_peers[0],
                device_id_type=MESH,
            ).wait_recv()
    high, low = split(trecv[...].reshape(sources * 64, 128))
    table[:, 0:128] = high
    table[:, 128:256] = low
    key_lane = lax.broadcasted_iota(jnp.int32, (units, sources * 64), 1).astype(F32)
    lane256 = lax.broadcasted_iota(jnp.int32, (units, 256), 1)
    low_lane = ((lane256 // 4) % 4).astype(F32)
    slot_of = (lane256 // 16) % 8
    picked = jnp.zeros((units, 256), F32)
    for m in range(SLOTS):
        hot = jnp.where(key[:, m : m + 1] == key_lane, 1.0, 0.0).astype(BF16)
        found = dot(hot, table[...])
        found = jnp.where(low_lane == tile_low[:, m : m + 1], found, 0.0).astype(BF16)
        picked = jnp.where(slot_of == m, dot(found, cbuf[0:256, :]), picked)
    high, low = split(picked)
    pb[0] = high[:, 0:128]
    pb[1] = high[:, 128:256]
    pb[2] = low[:, 0:128]
    pb[3] = low[:, 128:256]
    loaded("weights")
    own_tile = lax.broadcasted_iota(jnp.int32, (16, 256), 0) == (
        lax.broadcasted_iota(jnp.int32, (16, 256), 1) // 16
    )
    for g in range(16):
        left = pb[:, 16 * g : 16 * g + 16, :].reshape(64, 128)
        right = wbuf[g // 2, 16 * (g % 2) : 16 * (g % 2) + 16].reshape(256, 128)
        out = lax.dot_general(
            left, right, (((1,), (1,)), ((), ())), preferred_element_type=F32
        )
        for f in range(2):
            value = out[16 * f : 16 * f + 16] + out[32 + 16 * f : 48 + 16 * f]
            value = jnp.sum(jnp.where(own_tile, value, 0.0), axis=0, keepdims=True)
            for u in range(2):
                dbuf[f, 2 * (g % 2) + u, g // 2 : g // 2 + 1, :] = value[:, 128 * u : 128 * u + 128]
    high, low = split(dbuf[...].reshape(64, 128))
    turned = dot(jnp.concatenate([high, low], axis=0), cbuf[512:640, 0:128])
    turned = turned[:64] + turned[64:]
    for f in range(2):
        quarters = [turned[32 * f + 8 * q : 32 * f + 8 * q + 8] for q in range(4)]
        for dx in range(4):
            acc = jnp.zeros((8, 128), F32)
            for q in range(4):
                shift = ((q - dx) * 32) % 128
                moved = pltpu.roll(quarters[q], shift, 1) if shift else quarters[q]
                acc = jnp.where(lane128 // 32 == q, moved, acc)
            imp[f, pl.ds(dx, 8, stride=4), :] = acc

    wet_c = grid[4]
    heat = jnp.where(is_ocean, -(wet_c * imp[0]), grid[0])
    cells = jnp.where(is_ocean, wet_c, 0.0)
    row8 = lax.broadcasted_iota(jnp.int32, (8, 128), 0)

    def rows8(v):
        return jnp.sum(v, axis=0, keepdims=True)

    red[0] = jnp.where(row8 == 0, rows8(heat), jnp.where(row8 == 1, rows8(cells), 0.0))

    def sum_copy(phase, j):
        return pltpu.make_async_remote_copy(
            src_ref=red.at[phase],
            dst_ref=redr.at[phase, j],
            send_sem=rs.at[phase, j],
            recv_sem=rr.at[phase, j],
            device_id=sum_phases[phase][j],
            device_id_type=MESH,
        )

    def sum_send(phase):
        for j in range(len(sum_phases[phase])):
            sum_copy(phase, j).start()

    def sum_finish(phase):
        total = red[phase]
        for j in range(len(sum_phases[phase])):
            sum_copy(phase, j).wait_recv()
            total = total + redr[phase, j]
        red[phase + 1] = total

    sum_send(0)

    centre = (bound_high + bound_low) / 2.0
    half_range = (bound_high - bound_low) / 2.0
    spread_ratio = centre / half_range

    def apply_a(s, center):
        rim_row(SURF, 5)
        east, west, north, south = shifted(center, *side_rows(s, SURF), grid[5])
        near = coef[6] * east + coef[7] * west + coef[8] * north + coef[9] * south
        return wet_c * (coef[10] * center - near) + (1.0 - wet_c) * center

    def put_surface(s, value):
        grid[13] = value
        if s < ITERS:
            for x in range(CX):
                fp[s, x + 1, SURF : SURF + 1, :] = grid[13, x : x + 1, :]

    @pl.when(is_ocean)
    def _():
        force = heat_rate * wet_c * imp[0]
        grid[7] = force
        for x in range(CX):
            fp[1, x + 1, 0:1, :] = fp[1, x + 1, 0:1, :] + grid[7, x : x + 1, :]
        send(1, SLAB)
        pack_edge(1, LEVELS)
        send(1, OUTER)
        pack_inner(1, INNER, LEVELS)
        send(1, INSIDE)
        eta = grid[1]
        residual = wet_c * (damping * eta + fresh_rate * imp[1]) - apply_a(0, eta)
        direction = solve(residual) / centre
        grid[11] = eta + direction
        grid[12] = residual
        put_surface(1, direction)
        send(1, SLAB_SURF)
        pack_inner(1, ALL, (6,))
        send(1, SURF_COLUMN)

    @pl.when(is_air)
    def _():
        grid[6] = air_rate * imp[0]
        grid[7] = air_rate * imp[1]
        grid[10] = press_rate * imp[0]
        grid[5] = grid[6] - grid[7] * grid[8]
        grid[11] = grid[10] - press_rate * grid[9]
        for x in range(CX):
            fp[1, x + 1, 0:1, :] = fp[1, x + 1, 0:1, :] + grid[5, x : x + 1, :]
            fp[1, x + 1, SURF : SURF + 1, :] = (
                fp[1, x + 1, SURF : SURF + 1, :] + grid[11, x : x + 1, :]
            )
        send(1, SLAB, SLAB_SURF)
        pack_edge(1, BOTH)
        send(1, CORNER, OUTER)
        pack_inner(1, INNER, BOTH)
        send(1, INSIDE, SURF_COLUMN)

    recurrence = 1.0 / spread_ratio
    phases = len(sum_phases)
    for s in range(2, NSTEP + 1):
        last = s == NSTEP
        recurrence_next = 1.0 / (2.0 * spread_ratio - recurrence)

        @pl.when(is_ocean)
        def _(s=s, last=last, recurrence=recurrence, recurrence_next=recurrence_next):
            wait(s - 1, INSIDE)
            unpack_inner(s - 1, INNER, LEVELS)
            ocean_step(s, INNER)
            if not last:
                pack_inner(s, INNER, LEVELS)
                send(s, INSIDE)
            if s <= ITERS:
                wait(s - 1, SURF_COLUMN, SLAB_SURF)
                unpack_inner(s - 1, ALL, (6,))
                old = grid[13]
                residual = grid[12] - apply_a(s - 1, old)
                direction = (recurrence_next * recurrence) * old + (
                    2.0 * recurrence_next / half_range
                ) * solve(residual)
                grid[11] = grid[11] + direction
                grid[12] = residual
                put_surface(s, direction)
                if s < ITERS:
                    send(s, SLAB_SURF)
                    pack_inner(s, ALL, (6,))
                    send(s, SURF_COLUMN)
            wait(s - 1, OUTER, SLAB)
            unpack_edge(s - 1, LEVELS)
            ocean_step(s, EDGE)
            if not last:
                send(s, SLAB)
                pack_edge(s, LEVELS)
                send(s, OUTER)

        @pl.when(is_air)
        def _(s=s, last=last):
            used = BOTH if s <= ITERS else LEVELS
            made = BOTH if s < ITERS else LEVELS
            wait(s - 1, INSIDE, OUTER)
            if s <= ITERS:
                wait(s - 1, SURF_COLUMN)
            unpack_inner(s - 1, INNER, used)
            unpack_edge(s - 1, used)
            air_step(s, tuple(range(1, CX // 4 - 1)))
            if not last:
                pack_inner(s, INNER, made)
                send(s, INSIDE)
                if s < ITERS:
                    send(s, SURF_COLUMN)
            wait(s - 1, SLAB, CORNER)
            if s <= ITERS:
                wait(s - 1, SLAB_SURF)
            unpack_corner(s - 1, used)
            air_step(s, (0, CX // 4 - 1))
            if not last:
                send(s, SLAB)
                if s < ITERS:
                    send(s, SLAB_SURF)
                pack_edge(s, made)
                send(s, CORNER, OUTER)
            if s == ITERS:
                gather_row(s, SURF, 11)

        recurrence = recurrence_next
        if s == ITERS:
            loads["surface"] = [pltpu.make_async_copy(grid.at[11], surface_out.at[0], lsem.at[41])]
            loads["surface"][0].start()
        phase = s - 2
        if phase < phases:
            sum_finish(phase)
            if phase + 1 < phases:
                sum_send(phase + 1)

    total = red[phases]
    correction = jnp.sum(total[0:1, :], axis=1, keepdims=True) / jnp.sum(
        total[1:2, :], axis=1, keepdims=True
    )
    response = heat_response()

    @pl.when(is_ocean)
    def _():
        spread = jnp.zeros((8, 128), F32)
        for k in range(NSTEP):
            spread = jnp.where(row8 == k, response[k], spread)
        spread = spread * correction

        def body(x, carry):
            fp[NSTEP, x + 1, 0:8, :] = (
                fp[NSTEP, x + 1, 0:8, :] + spread * grid[4, pl.ds(x, 1), :]
            )
            return carry

        lax.fori_loop(0, CX, body, 0)

    stores = []
    for x in range(CX):
        copy = pltpu.make_async_copy(
            fp.at[NSTEP, x + 1, pl.ds(0, LEV), :], theta_out.at[0, :, x, :], lsem.at[8 + x]
        )
        copy.start()
        stores.append(copy)
    for s in range(NSTEP):
        drain_halo(s)
    for d, j, peer in export_peers:
        export_copy(d, j, peer).wait_send()
    for phase in range(phases):
        for j in range(len(sum_phases[phase])):
            sum_copy(phase, j).wait_send()
    loaded("surface")
    for copy in stores:
        copy.wait()


def solution(mesh):
    n_gx = mesh.shape["gx"]
    n_gy = mesh.shape["gy"]
    sources = 3 * n_gy
    phases = 1 + len(radices(n_gx))
    widest = max(2 * n_gy - 1, 3)
    constants = tables()

    def per_device(theta, surface, kappa, depth, wet, ids, counts, weights):
        spec = pl.BlockSpec(memory_space=pl.ANY)
        dma = pltpu.SemaphoreType.DMA
        return pl.pallas_call(
            functools.partial(kernel, n_gx, n_gy),
            out_shape=(
                jax.ShapeDtypeStruct((1, LEV, CX, CY), F32),
                jax.ShapeDtypeStruct((1, CX, CY), F32),
            ),
            in_specs=[spec] * 9,
            out_specs=(spec, spec),
            scratch_shapes=[
                pltpu.VMEM((NSTEP + 1, CX + 2, ROWS, CY), F32),
                pltpu.VMEM((NSTEP, 4, 8, CY), F32),
                pltpu.VMEM((NSTEP, 2, 4, 8, CY), F32),
                pltpu.VMEM((NSTEP, 8, CY), F32),
                pltpu.VMEM((NSTEP, 6, 8, CY), F32),
                pltpu.VMEM((CX + 2, ROWS, CY), F32),
                pltpu.VMEM((2, CX, CY), F32),
                pltpu.VMEM((64, 128), F32),
                pltpu.VMEM((sources, 64, 128), F32),
                pltpu.VMEM((sources * 64, 256), BF16),
                pltpu.VMEM((8, 32, 16, 128), BF16),
                pltpu.VMEM((640, 256), BF16),
                pltpu.VMEM((8, SLOTS, 32), jnp.int32),
                pltpu.VMEM((8, 32), jnp.int32),
                pltpu.VMEM((CX, CY), jnp.int32),
                pltpu.VMEM((11, CX, CY), F32),
                pltpu.VMEM((4, 256, 128), BF16),
                pltpu.VMEM((2, 4, 8, 128), F32),
                pltpu.VMEM((2, CX, CY), F32),
                pltpu.VMEM((15, CX, CY), F32),
                pltpu.VMEM((14, CX, CY), F32),
                pltpu.VMEM((phases + 1, 8, 128), F32),
                pltpu.VMEM((phases, widest, 8, 128), F32),
                dma((42,)),
                dma((NSTEP, 14)),
                dma((NSTEP, 14)),
                dma((sources,)),
                dma((sources,)),
                dma((phases, widest)),
                dma((phases, widest)),
            ],
            compiler_params=pltpu.CompilerParams(
                collective_id=0, has_side_effects=True, vmem_limit_bytes=60 * 1024 * 1024
            ),
        )(
            theta,
            surface,
            kappa,
            depth,
            wet,
            ids.transpose(0, 1, 3, 2),
            counts,
            weights,
            jnp.asarray(constants),
        )

    in_specs = (
        P("comp", None, "gx", "gy"),
        P("comp", "gx", "gy"),
        P("comp", "gx", "gy"),
        P("gx", "gy"),
        P("gx", "gy"),
        P("comp", "gx", "gy", None),
        P("comp", "gx", "gy"),
        P("comp", "gx", "gy", None, None),
    )
    out_specs = (P("comp", None, "gx", "gy"), P("comp", "gx", "gy"))
    return jax.shard_map(
        per_device, mesh=mesh, in_specs=in_specs, out_specs=out_specs, check_vma=False
    )
```

```python
import functools

import jax
import jax.numpy as jnp
import ml_dtypes
import numpy as np
from jax import lax
from jax.experimental import pallas as pl
from jax.experimental.pallas import tpu as pltpu
from jax.sharding import PartitionSpec as P

MESH = pl.DeviceIdType.MESH
F32 = jnp.float32
BF16 = jnp.bfloat16

NSTEP = 6
ITERS = 4
SLOTS = 8
LEV = 48
CX = 32
CY = 128
ROWS = 56
SURF = 48
EDGE = (0, 1, 2, 3, 28, 29, 30, 31)
INNER = tuple(range(4, 28))

node_derivative = np.array(
    [
        [-3.0, 4.045084971874737, -1.545084971874737, 0.5],
        [-0.809016994374947, 0.0, 1.118033988749895, -0.309016994374947],
        [0.309016994374947, -1.118033988749895, 0.0, 0.809016994374947],
        [-0.5, 1.545084971874737, -4.045084971874737, 3.0],
    ]
)
second_derivative = node_derivative @ node_derivative
vertical_mix = 0.2
heat_rate = 0.5
air_rate = 0.3
press_rate = 0.1
damping = 0.05
fresh_rate = 0.5
bound_low = 0.02
bound_high = 2.0


def heat_response():
    level = np.zeros(LEV)
    for _ in range(NSTEP):
        change = level[1:] - level[:-1]
        level = level + vertical_mix * (np.append(change, 0.0) - np.append(0.0, change))
        level[0] += heat_rate
    return [float(v) for v in level]


def halves(table):
    high = table.astype(ml_dtypes.bfloat16)
    low = (table - high.astype(np.float64)).astype(ml_dtypes.bfloat16)
    return high, low


def tables():
    lane = np.arange(256)
    f_in, dx_in, dy_in = (lane // 64) % 2, (lane // 16) % 4, lane % 4
    f_out, dx_out, dy_out = lane // 128, (lane // 4) % 4, lane % 4
    fold = (
        (f_in[:, None] == f_out[None])
        & (dx_in[:, None] == dx_out[None])
        & (dy_in[:, None] == dy_out[None])
    )
    block = np.kron(np.eye(32), second_derivative.T)
    high, low = halves(block)
    zero = np.zeros((128, 128))
    lap = np.block(
        [[high.astype(np.float64), low.astype(np.float64)], [high.astype(np.float64), zero]]
    )
    lane = np.arange(128)
    target = ((lane // 4) % 4) * 32 + (lane // 16) * 4 + lane % 4
    perm = np.zeros((128, 256))
    perm[lane, target] = 1.0
    return np.concatenate([fold.astype(np.float64), lap, perm]).astype(ml_dtypes.bfloat16)


def split(value):
    high = value.astype(BF16)
    low = (value - high.astype(F32)).astype(BF16)
    return high, low


def dot(a, b):
    return jnp.dot(a, b, preferred_element_type=F32)


def radices(count):
    if count == 32:
        return [4, 2, 4]
    found = []
    while count > 1:
        size = 4 if count % 4 == 0 else count
        found.append(size)
        count //= size
    return found


def kernel(
    n_gx,
    n_gy,
    theta,
    surface,
    kappa,
    depth,
    wet,
    ids,
    counts,
    weights,
    consts,
    fin,
    surface_fin,
    fp,
    ys,
    yr,
    ye,
    yer,
    zb,
    ex,
    tsend,
    trecv,
    table,
    wbuf,
    cbuf,
    idbuf,
    cntbuf,
    wetbuf,
    coef,
    pb,
    hot,
    dbuf,
    imp,
    pcr,
    grid,
    red,
    redr,
    lsem,
    hs,
    hr,
    es,
    er,
    rs,
    rr,
):
    comp = lax.axis_index("comp")
    gx = lax.axis_index("gx")
    gy = lax.axis_index("gy")
    sources = 3 * n_gy
    units = (CX // 4) * (CY // 4)
    is_ocean = comp == 0
    is_air = comp == 1
    has_south = gy > 0
    has_north = gy < n_gy - 1

    def place(dc, dx, dy):
        return (lax.rem(comp + dc, 2), lax.rem(gx + dx + n_gx, n_gx), lax.rem(gy + dy + n_gy, n_gy))

    halo_peers = [
        place(0, 1, 0),
        place(0, -1, 0),
        place(0, 0, 1),
        place(0, 0, -1),
        place(0, 1, 1),
        place(0, -1, 1),
        place(0, 1, -1),
        place(0, -1, -1),
    ]
    export_peers = [(d, j, place(1, d, j)) for d in (-1, 0, 1) for j in range(n_gy)]
    sum_phases = []
    sum_phases.append([place(dc, 0, j) for dc in range(2) for j in range(n_gy) if dc or j])
    stride = 1
    for size in radices(n_gx):
        digit = lax.rem(gx // stride, size)
        group = []
        for j in range(1, size):
            group.append((comp, gx + (lax.rem(digit + j, size) - digit) * stride, gy))
        sum_phases.append(group)
        stride *= size

    barrier = pltpu.get_barrier_semaphore()
    greeted = halo_peers + [p for _, _, p in export_peers] + [p for g in sum_phases for p in g]
    for peer in greeted:
        pl.semaphore_signal(barrier, inc=1, device_id=peer, device_id_type=MESH)

    loads = {}

    def load(name, index, src, dst):
        copy = pltpu.make_async_copy(src, dst, lsem.at[index])
        copy.start()
        loads.setdefault(name, []).append(copy)

    def loaded(name):
        for copy in loads.pop(name):
            copy.wait()

    load("export", 0, theta.at[0, 0], grid.at[0])
    load("export", 1, surface.at[0], grid.at[1])
    load("export", 2, wet, wetbuf)
    load("export", 3, kappa.at[0], grid.at[2])
    load("export", 4, depth, grid.at[3])
    for x in range(CX):
        load("theta", 8 + x, theta.at[0, :, x, :], fp.at[0, x + 1, pl.ds(0, LEV), :])
    load("remap", 5, ids.at[0], idbuf)
    load("remap", 6, counts.at[0], cntbuf)
    load("tables", 7, consts, cbuf)
    load("weights", 40, weights.at[0], wbuf)

    lane128 = lax.broadcasted_iota(jnp.int32, (8, 128), 1)
    lane1 = lax.broadcasted_iota(jnp.int32, (1, 128), 1)

    loaded("export")
    wet_float = wetbuf[...].astype(F32)
    grid[4] = wet_float
    top = grid[0]

    ex[0] = jnp.where(is_ocean, top * wet_float, top)
    ex[1] = jnp.where(is_ocean, wet_float, grid[1])
    parts = [ex[f, pl.ds(dx, 8, stride=4), :] for f in range(2) for dx in range(4)]
    for h in range(8):
        acc = jnp.zeros((8, 128), F32)
        for j in range(8):
            shift = ((j - h) * 16) % 128
            moved = pltpu.roll(parts[j], shift, 1) if shift else parts[j]
            acc = jnp.where(lane128 // 16 == j, moved, acc)
        tsend[pl.ds(8 * h, 8), :] = acc

    for x in range(CX):
        fp[0, x + 1, SURF : SURF + 1, :] = grid[1, x : x + 1, :]
        fp[0, x + 1, SURF + 1 : SURF + 2, :] = grid[2, x : x + 1, :]
        fp[0, x + 1, SURF + 2 : SURF + 3, :] = grid[3, x : x + 1, :]
        fp[0, x + 1, SURF + 3 : SURF + 4, :] = grid[4, x : x + 1, :]
        fp[0, x + 1, SURF + 4 : SURF + 8, :] = jnp.zeros((4, 128), F32)

    def place_in(acc, moved, lane):
        return jnp.where((lane128 == lane) | (lane128 == lane + 1), moved, acc)

    def pack_inner(s, slabs, blocks):
        for j in range(4):
            acc = jnp.zeros((8, 128), F32)
            found = False
            for b in (2 * j, 2 * j + 1):
                if b in blocks:
                    found = True
                    for x in slabs:
                        lane = 2 * x + 64 * (b % 2)
                        moved = pltpu.roll(fp[s, x + 1, 8 * b : 8 * b + 8, :], (lane + 1) % 128, 1)
                        acc = place_in(acc, moved, lane)
            if found:
                ys[s, j] = acc

    def pack_edge(s, blocks):
        acc = jnp.zeros((8, 128), F32)
        for b in blocks:
            for e, x in enumerate(EDGE):
                lane = 16 * b + 2 * e
                moved = pltpu.roll(fp[s, x + 1, 8 * b : 8 * b + 8, :], lane + 1, 1)
                acc = place_in(acc, moved, lane)
        ye[s] = acc

    def merge(low, high):
        return jnp.where(lane128 % 2 == 0, low, pltpu.roll(high, 126, 1))

    def turn(value, lane):
        return pltpu.roll(value, (128 - lane) % 128, 1) if lane % 128 else value

    def unpack_inner(s, slabs, blocks):
        for j in range(4):
            if 2 * j in blocks or 2 * j + 1 in blocks:
                both = merge(yr[s, 0, j], yr[s, 1, j])
                for b in (2 * j, 2 * j + 1):
                    if b in blocks:
                        for x in slabs:
                            zb[x + 1, 8 * b : 8 * b + 8, :] = turn(both, 2 * x + 64 * (b % 2))

    def unpack_edge(s, blocks):
        both = merge(yer[s, 0], yer[s, 1])
        for b in blocks:
            for e, x in enumerate(EDGE):
                zb[x + 1, 8 * b : 8 * b + 8, :] = turn(both, 16 * b + 2 * e)

    def unpack_corner(s, blocks):
        west = merge(yer[s, 2], yer[s, 4])
        east = merge(yer[s, 3], yer[s, 5])
        for b in blocks:
            zb[0, 8 * b : 8 * b + 8, :] = turn(west, 16 * b + 14)
            zb[CX + 1, 8 * b : 8 * b + 8, :] = turn(east, 16 * b)

    def copy_to(s, d):
        peer = halo_peers[d % 2 if d < 4 else 2 + d % 2 if d < 10 else d - 6]
        if d < 4:
            rows = pl.ds(0, LEV) if d < 2 else pl.ds(SURF, 8)
            src = fp.at[s, CX if d % 2 == 0 else 1, rows, :]
            dst = fp.at[s, 0 if d % 2 == 0 else CX + 1, rows, :]
        elif d < 6:
            src, dst = ye.at[s], yer.at[s, d - 4]
        elif d < 8:
            src, dst = ys.at[s, pl.ds(0, 3)], yr.at[s, d - 6, pl.ds(0, 3)]
        elif d < 10:
            src, dst = ys.at[s, 3], yr.at[s, d - 8, 3]
        else:
            src, dst = ye.at[s], yer.at[s, d - 8]
        return pltpu.make_async_remote_copy(
            src_ref=src,
            dst_ref=dst,
            send_sem=hs.at[s, d],
            recv_sem=hr.at[s, d],
            device_id=peer,
            device_id_type=MESH,
        )

    SLAB, SLAB_SURF, OUTER, INSIDE, SURF_COLUMN = (0, 1), (2, 3), (4, 5), (6, 7), (8, 9)
    CORNER = (10, 11, 12, 13)

    def send(s, *kinds):
        for kind in kinds:
            for d in kind:
                copy_to(s, d).start()

    def wait(s, *kinds):
        for kind in kinds:
            for d in kind:
                copy_to(s, d).wait_recv()

    def drain_halo(s):
        kinds = [SLAB, OUTER, INSIDE]
        if s < ITERS:
            kinds += [SLAB_SURF, SURF_COLUMN]
        for kind in kinds:
            for d in kind:
                copy_to(s, d).wait_send()

        @pl.when(is_air)
        def _():
            for d in CORNER:
                copy_to(s, d).wait_send()

    def export_copy(d, j, peer):
        slot = (1 - d) * n_gy + gy
        return pltpu.make_async_remote_copy(
            src_ref=tsend,
            dst_ref=trecv.at[slot],
            send_sem=es.at[(d + 1) * n_gy + j],
            recv_sem=er.at[slot],
            device_id=peer,
            device_id_type=MESH,
        )

    ALL = tuple(range(CX))
    LEVELS = tuple(range(6))
    BOTH = tuple(range(7))
    loaded("theta")
    pack_edge(0, BOTH)
    pack_inner(0, INNER, LEVELS)
    pack_inner(0, ALL, (6,))
    pl.semaphore_wait(barrier, len(greeted))
    send(0, SLAB, SLAB_SURF, OUTER)

    @pl.when(is_air)
    def _():
        send(0, CORNER)

    send(0, INSIDE, SURF_COLUMN)
    for d, j, peer in export_peers:
        if d:
            export_copy(d, j, peer).start()
    for d, j, peer in export_peers:
        if not d:
            export_copy(d, j, peer).start()

    loaded("remap")
    loaded("tables")
    gy_bits = n_gy.bit_length() - 1
    id_all = idbuf[...]
    unit = id_all & (units - 1)
    dev = id_all >> 8
    dev_gy = dev & (n_gy - 1)
    offset = (dev >> gy_bits) - gx + 1
    offset = jnp.where(offset < 0, offset + n_gx, jnp.where(offset >= n_gx, offset - n_gx, offset))
    tile_y = unit & 31
    source = offset * n_gy + dev_gy
    row = (tile_y >> 2) * 8 + (unit >> 5)
    low_tile = tile_y & 3
    slot_order = lax.broadcasted_iota(jnp.int32, (8, SLOTS, 32), 1)
    source = jnp.where(slot_order < cntbuf[...][:, None, :], source, 200)
    eye = jnp.where(
        lax.broadcasted_iota(jnp.int32, (32, 32), 0) == lax.broadcasted_iota(jnp.int32, (32, 32), 1),
        1.0,
        0.0,
    ).astype(BF16)
    columns = []
    for tx in range(8):
        stacked = jnp.concatenate([source[tx], row[tx], low_tile[tx], low_tile[tx]], axis=0)
        columns.append(
            lax.dot_general(
                eye,
                stacked.astype(F32).astype(BF16),
                (((1,), (1,)), ((), ())),
                preferred_element_type=F32,
            )
        )
    columns = jnp.concatenate(columns, axis=0)
    key = columns[:, 0:8] * 64.0 + columns[:, 8:16]
    tile_low = columns[:, 16:24]
    key_lane = lax.broadcasted_iota(jnp.int32, (units, sources * 64), 1).astype(F32)
    for m in range(SLOTS):
        hot[m] = jnp.where(key[:, m : m + 1] == key_lane, 1.0, 0.0).astype(BF16)

    wait(0, INSIDE, OUTER, SURF_COLUMN)
    unpack_inner(0, INNER, LEVELS)
    unpack_inner(0, ALL, (6,))
    unpack_edge(0, LEVELS)
    wait(0, SLAB, SLAB_SURF)

    @pl.when(is_air)
    def _():
        wait(0, CORNER)
        unpack_corner(0, BOTH)


    def lanes_of(shape):
        return lax.broadcasted_iota(jnp.int32, shape, 1)

    lane_full = lanes_of((CX, CY))

    def gather_row(s, row, slot):
        for x in range(CX):
            grid[slot, x : x + 1, :] = fp[s, x + 1, row : row + 1, :]

    def rim_row(row, slot):
        for x in range(CX):
            grid[slot, x : x + 1, :] = zb[x + 1, row : row + 1, :]

    def shifted(center, west_row, east_row, rim):
        row_place = lax.broadcasted_iota(jnp.int32, (CX, CY), 0)
        east = jnp.where(row_place == CX - 1, east_row, pltpu.roll(center, CX - 1, 0))
        west = jnp.where(row_place == 0, west_row, pltpu.roll(center, 1, 0))
        north = jnp.where(lane_full == CY - 1, rim, pltpu.roll(center, CY - 1, 1))
        south = jnp.where(lane_full == 0, rim, pltpu.roll(center, 1, 1))
        return east, west, north, south

    def side_rows(s, row):
        return fp[s, 0, row : row + 1, :], fp[s, CX + 1, row : row + 1, :]

    def wet_sides():
        wet_c = grid[4]
        rim_row(SURF + 3, 5)
        we, ww, wn, ws = shifted(wet_c, *side_rows(0, SURF + 3), grid[5])
        wn = jnp.where((lane_full == CY - 1) & jnp.logical_not(has_north), 0.0, wn)
        ws = jnp.where((lane_full == 0) & jnp.logical_not(has_south), 0.0, ws)
        return wet_c, we, ww, wn, ws

    def faces(row, slot, at):
        wet_c, we, ww, wn, ws = wet_sides()
        center = grid[slot]
        rim_row(row, 5)
        ke, kw, kn, ks = shifted(center, *side_rows(0, row), grid[5])
        base = center * wet_c
        coef[at] = 0.5 * (base + ke * we) * wet_c * we
        coef[at + 1] = 0.5 * (kw * ww + base) * ww * wet_c
        coef[at + 2] = 0.5 * (base + kn * wn) * wet_c * wn
        coef[at + 3] = 0.5 * (ks * ws + base) * ws * wet_c

    @pl.when(is_ocean)
    def _():
        faces(SURF + 1, 2, 0)
        wet_c = grid[4]
        coef[4] = (
            1.0 - (coef[0] + coef[1] + coef[2] + coef[3]) - (2.0 * vertical_mix) * wet_c
        )
        coef[5] = vertical_mix * wet_c

    def line_factors():
        faces(SURF + 2, 3, 6)
        wet_c = grid[4]
        diagonal = damping + coef[6] + coef[7] + coef[8] + coef[9]
        coef[10] = diagonal
        main = wet_c * diagonal + (1.0 - wet_c)
        lower = jnp.where(lane_full == 0, 0.0, -coef[9])
        upper = jnp.where(lane_full == CY - 1, 0.0, -coef[8])
        step = 1
        index = 0
        while step < CY:
            back = CY - step
            below_main = pltpu.roll(main, step, 1)
            above_main = pltpu.roll(main, back, 1)
            factor_below = -lower / below_main
            factor_above = -upper / above_main
            pcr[index] = factor_below
            pcr[index + 1] = factor_above
            main = (
                main
                + factor_below * pltpu.roll(upper, step, 1)
                + factor_above * pltpu.roll(lower, back, 1)
            )
            lower = factor_below * pltpu.roll(lower, step, 1)
            upper = factor_above * pltpu.roll(upper, back, 1)
            step *= 2
            index += 2
        pcr[14] = 1.0 / main

    def solve(values):
        step = 1
        index = 0
        while step < CY:
            values = (
                values
                + pcr[index] * pltpu.roll(values, step, 1)
                + pcr[index + 1] * pltpu.roll(values, CY - step, 1)
            )
            step *= 2
            index += 2
        return values * pcr[14]

    row48 = lax.broadcasted_iota(jnp.int32, (LEV, CY), 0)
    lane48 = lanes_of((LEV, CY))

    def out_ref(s, x):
        return fin.at[x] if s == NSTEP else fp.at[s, x + 1]

    def ocean_step(s, slabs):
        for x in slabs:
            c = fp[s - 1, x + 1, 0:LEV, :]
            w = fp[s - 1, x, 0:LEV, :]
            e = fp[s - 1, x + 2, 0:LEV, :]
            z = zb[x + 1, 0:LEV, :]

            def row(i, x=x):
                return coef[i, x : x + 1, :]

            n = jnp.where(lane48 == CY - 1, z, pltpu.roll(c, CY - 1, 1))
            o = jnp.where(lane48 == 0, z, pltpu.roll(c, 1, 1))
            up = jnp.where(row48 == LEV - 1, c, pltpu.roll(c, LEV - 1, 0))
            down = jnp.where(row48 == 0, c, pltpu.roll(c, 1, 0))
            new = (
                row(4) * c
                + row(0) * e
                + row(1) * w
                + row(2) * n
                + row(3) * o
                + row(5) * (up + down)
            )
            out_ref(s, x)[0:LEV, :] = new
            if s > 1:
                out_ref(s, x)[0:1, :] = new[0:1, :] + grid[7, x : x + 1, :]

    def air_step(s, tiles):
        rows = ROWS if s <= ITERS else LEV
        lane_r = lanes_of((rows, CY))
        row_r = lax.broadcasted_iota(jnp.int32, (rows, CY), 0)
        h = jnp.where(
            ((lane1 % 4 == 0) & ((lane1 > 0) | has_south))
            | ((lane1 % 4 == 3) & ((lane1 < CY - 1) | has_north)),
            0.5,
            0.0,
        )
        mix_up = jnp.where(row_r < LEV - 1, vertical_mix, 0.0)
        mix_down = jnp.where((row_r > 0) & (row_r < LEV), vertical_mix, 0.0)

        for i in tiles:
            x0 = 4 * i
            v = [fp[s - 1, x0 + j, 0:rows, :] for j in range(6)]
            z = [zb[x0 + j, 0:rows, :] for j in range(6)]

            def across(t):
                return [0.5 * (t[1] + t[0]), t[2], t[3], 0.5 * (t[4] + t[5])]

            blocks = []
            for a, za in zip(across(v), across(z)):
                partner = jnp.where(lane_r % 4 == 0, pltpu.roll(a, 1, 1), pltpu.roll(a, CY - 1, 1))
                partner = jnp.where((lane_r == 0) | (lane_r == CY - 1), za, partner)
                blocks.append(a + h * (partner - a))
            high, low = split(jnp.concatenate(blocks, axis=0))
            along = dot(jnp.concatenate([high, low], axis=1), cbuf[256:512, :])
            along = along[:, :CY] + along[:, CY:]
            for j in range(4):
                b = blocks[j]
                lap = along[rows * j : rows * (j + 1)]
                for m in range(4):
                    lap = lap + float(second_derivative[j, m]) * blocks[m]
                up = pltpu.roll(b, rows - 1, 0)
                down = pltpu.roll(b, 1, 0)
                new = (
                    b
                    + grid[2, x0 + j : x0 + j + 1, :] * lap
                    + mix_up * (up - b)
                    + mix_down * (down - b)
                )
                x = x0 + j
                out_ref(s, x)[0:rows, :] = new
                if s == 1:
                    grid[8, x : x + 1, :] = b[0:1, :]
                    grid[9, x : x + 1, :] = b[SURF : SURF + 1, :]
                else:
                    out_ref(s, x)[0:1, :] = (
                        new[0:1, :]
                        + grid[6, x : x + 1, :]
                        - grid[7, x : x + 1, :] * b[0:1, :]
                    )
                    if s <= ITERS:
                        fp[s, x + 1, SURF : SURF + 1, :] = (
                            new[SURF : SURF + 1, :]
                            + grid[10, x : x + 1, :]
                            - press_rate * b[SURF : SURF + 1, :]
                        )


    def apply_a(s, center):
        wet_c = grid[4]
        rim_row(SURF, 5)
        east, west, north, south = shifted(center, *side_rows(s, SURF), grid[5])
        near = coef[6] * east + coef[7] * west + coef[8] * north + coef[9] * south
        return wet_c * (coef[10] * center - near) + (1.0 - wet_c) * center

    @pl.when(is_ocean)
    def _():
        ocean_step(1, ALL)
        line_factors()
        grid[8] = apply_a(0, grid[1])

    @pl.when(is_air)
    def _():
        unpack_edge(0, (6,))
        air_step(1, tuple(range(CX // 4)))

    for d in range(3):
        for j in range(n_gy):
            slot = d * n_gy + j
            pltpu.make_async_remote_copy(
                src_ref=tsend,
                dst_ref=trecv.at[slot],
                send_sem=es.at[slot],
                recv_sem=er.at[slot],
                device_id=halo_peers[0],
                device_id_type=MESH,
            ).wait_recv()
    high, low = split(trecv[...].reshape(sources * 64, 128))
    table[:, 0:128] = high
    table[:, 128:256] = low
    lane256 = lax.broadcasted_iota(jnp.int32, (units, 256), 1)
    low_lane = ((lane256 // 4) % 4).astype(F32)
    slot_of = (lane256 // 16) % 8
    picked = jnp.zeros((units, 256), F32)
    for m in range(SLOTS):
        found = dot(hot[m], table[...])
        found = jnp.where(low_lane == tile_low[:, m : m + 1], found, 0.0).astype(BF16)
        picked = jnp.where(slot_of == m, dot(found, cbuf[0:256, :]), picked)
    high, low = split(picked)
    pb[0] = high[:, 0:128]
    pb[1] = high[:, 128:256]
    pb[2] = low[:, 0:128]
    pb[3] = low[:, 128:256]
    loaded("weights")
    own_tile = lax.broadcasted_iota(jnp.int32, (16, 256), 0) == (
        lax.broadcasted_iota(jnp.int32, (16, 256), 1) // 16
    )
    for g in range(16):
        left = pb[:, 16 * g : 16 * g + 16, :].reshape(64, 128)
        right = wbuf[g // 2, 16 * (g % 2) : 16 * (g % 2) + 16].reshape(256, 128)
        out = lax.dot_general(
            left, right, (((1,), (1,)), ((), ())), preferred_element_type=F32
        )
        for f in range(2):
            value = out[16 * f : 16 * f + 16] + out[32 + 16 * f : 48 + 16 * f]
            value = jnp.sum(jnp.where(own_tile, value, 0.0), axis=0, keepdims=True)
            for u in range(2):
                dbuf[f, 2 * (g % 2) + u, g // 2 : g // 2 + 1, :] = value[:, 128 * u : 128 * u + 128]
    high, low = split(dbuf[...].reshape(64, 128))
    turned = dot(jnp.concatenate([high, low], axis=0), cbuf[512:640, 0:128])
    turned = turned[:64] + turned[64:]
    for f in range(2):
        quarters = [turned[32 * f + 8 * q : 32 * f + 8 * q + 8] for q in range(4)]
        for dx in range(4):
            acc = jnp.zeros((8, 128), F32)
            for q in range(4):
                shift = ((q - dx) * 32) % 128
                moved = pltpu.roll(quarters[q], shift, 1) if shift else quarters[q]
                acc = jnp.where(lane128 // 32 == q, moved, acc)
            imp[f, pl.ds(dx, 8, stride=4), :] = acc

    wet_c = grid[4]
    heat = jnp.where(is_ocean, -(wet_c * imp[0]), grid[0])
    cells = jnp.where(is_ocean, wet_c, 0.0)
    row8 = lax.broadcasted_iota(jnp.int32, (8, 128), 0)

    def rows8(v):
        return jnp.sum(v, axis=0, keepdims=True)

    red[0] = jnp.where(row8 == 0, rows8(heat), jnp.where(row8 == 1, rows8(cells), 0.0))

    def sum_copy(phase, j):
        return pltpu.make_async_remote_copy(
            src_ref=red.at[phase],
            dst_ref=redr.at[phase, j],
            send_sem=rs.at[phase, j],
            recv_sem=rr.at[phase, j],
            device_id=sum_phases[phase][j],
            device_id_type=MESH,
        )

    def sum_send(phase):
        for j in range(len(sum_phases[phase])):
            sum_copy(phase, j).start()

    def sum_finish(phase):
        total = red[phase]
        for j in range(len(sum_phases[phase])):
            sum_copy(phase, j).wait_recv()
            total = total + redr[phase, j]
        red[phase + 1] = total

    sum_send(0)

    centre = (bound_high + bound_low) / 2.0
    half_range = (bound_high - bound_low) / 2.0
    spread_ratio = centre / half_range

    def put_surface(s, value):
        grid[13] = value
        if s < ITERS:
            for x in range(CX):
                fp[s, x + 1, SURF : SURF + 1, :] = grid[13, x : x + 1, :]

    @pl.when(is_ocean)
    def _():
        force = heat_rate * wet_c * imp[0]
        grid[7] = force
        for x in range(CX):
            fp[1, x + 1, 0:1, :] = fp[1, x + 1, 0:1, :] + grid[7, x : x + 1, :]
        send(1, SLAB)
        pack_edge(1, LEVELS)
        send(1, OUTER)
        pack_inner(1, INNER, LEVELS)
        send(1, INSIDE)
        eta = grid[1]
        residual = wet_c * (damping * eta + fresh_rate * imp[1]) - grid[8]
        direction = solve(residual) / centre
        grid[11] = eta + direction
        grid[12] = residual
        put_surface(1, direction)
        send(1, SLAB_SURF)
        pack_inner(1, ALL, (6,))
        send(1, SURF_COLUMN)

    @pl.when(is_air)
    def _():
        grid[6] = air_rate * imp[0]
        grid[7] = air_rate * imp[1]
        grid[10] = press_rate * imp[0]
        grid[5] = grid[6] - grid[7] * grid[8]
        grid[11] = grid[10] - press_rate * grid[9]
        for x in range(CX):
            fp[1, x + 1, 0:1, :] = fp[1, x + 1, 0:1, :] + grid[5, x : x + 1, :]
            fp[1, x + 1, SURF : SURF + 1, :] = (
                fp[1, x + 1, SURF : SURF + 1, :] + grid[11, x : x + 1, :]
            )
        send(1, SLAB, SLAB_SURF)
        pack_edge(1, BOTH)
        send(1, CORNER, OUTER)
        pack_inner(1, INNER, BOTH)
        send(1, INSIDE, SURF_COLUMN)

    recurrence = 1.0 / spread_ratio
    phases = len(sum_phases)
    for s in range(2, NSTEP + 1):
        last = s == NSTEP
        recurrence_next = 1.0 / (2.0 * spread_ratio - recurrence)

        @pl.when(is_ocean)
        def _(s=s, last=last, recurrence=recurrence, recurrence_next=recurrence_next):
            wait(s - 1, INSIDE)
            unpack_inner(s - 1, INNER, LEVELS)
            ocean_step(s, INNER)
            if not last:
                pack_inner(s, INNER, LEVELS)
                send(s, INSIDE)
            if s <= ITERS:
                wait(s - 1, SURF_COLUMN, SLAB_SURF)
                unpack_inner(s - 1, ALL, (6,))
                old = grid[13]
                residual = grid[12] - apply_a(s - 1, old)
                direction = (recurrence_next * recurrence) * old + (
                    2.0 * recurrence_next / half_range
                ) * solve(residual)
                grid[11] = grid[11] + direction
                grid[12] = residual
                put_surface(s, direction)
                if s < ITERS:
                    send(s, SLAB_SURF)
                    pack_inner(s, ALL, (6,))
                    send(s, SURF_COLUMN)
            wait(s - 1, OUTER, SLAB)
            unpack_edge(s - 1, LEVELS)
            ocean_step(s, EDGE)
            if not last:
                send(s, SLAB)
                pack_edge(s, LEVELS)
                send(s, OUTER)

        @pl.when(is_air)
        def _(s=s, last=last):
            used = BOTH if s <= ITERS else LEVELS
            made = BOTH if s < ITERS else LEVELS
            wait(s - 1, INSIDE, OUTER)
            if s <= ITERS:
                wait(s - 1, SURF_COLUMN)
            unpack_inner(s - 1, INNER, used)
            unpack_edge(s - 1, used)
            air_step(s, tuple(range(1, CX // 4 - 1)))
            if not last:
                pack_inner(s, INNER, made)
                send(s, INSIDE)
                if s < ITERS:
                    send(s, SURF_COLUMN)
            wait(s - 1, SLAB, CORNER)
            if s <= ITERS:
                wait(s - 1, SLAB_SURF)
            unpack_corner(s - 1, used)
            air_step(s, (0, CX // 4 - 1))
            if not last:
                send(s, SLAB)
                if s < ITERS:
                    send(s, SLAB_SURF)
                pack_edge(s, made)
                send(s, CORNER, OUTER)
            if s == ITERS:
                gather_row(s, SURF, 11)

        recurrence = recurrence_next
        phase = s - 2
        if phase < phases:
            sum_finish(phase)
            if phase + 1 < phases:
                sum_send(phase + 1)

    total = red[phases]
    correction = jnp.sum(total[0:1, :], axis=1, keepdims=True) / jnp.sum(
        total[1:2, :], axis=1, keepdims=True
    )
    response = heat_response()

    @pl.when(is_ocean)
    def _():
        spread = jnp.zeros((8, 128), F32)
        for k in range(NSTEP):
            spread = jnp.where(row8 == k, response[k], spread)
        spread = spread * correction

        for x in range(CX):
            fin[x, 0:8, :] = fin[x, 0:8, :] + spread * grid[4, x : x + 1, :]

    surface_fin[...] = grid[11]
    for s in range(NSTEP):
        drain_halo(s)
    for d, j, peer in export_peers:
        export_copy(d, j, peer).wait_send()
    for phase in range(phases):
        for j in range(len(sum_phases[phase])):
            sum_copy(phase, j).wait_send()


def store_kernel(fin, surface_fin, theta_out, surface_out, sem):
    copies = [pltpu.make_async_copy(surface_fin, surface_out.at[0], sem.at[CX])]
    for x in range(CX):
        copies.append(pltpu.make_async_copy(fin.at[x], theta_out.at[0, :, x, :], sem.at[x]))
    for copy in copies:
        copy.start()
    for copy in copies:
        copy.wait()


def solution(mesh):
    n_gx = mesh.shape["gx"]
    n_gy = mesh.shape["gy"]
    sources = 3 * n_gy
    phases = 1 + len(radices(n_gx))
    widest = max(2 * n_gy - 1, 3)
    constants = tables()

    def per_device(theta, surface, kappa, depth, wet, ids, counts, weights):
        spec = pl.BlockSpec(memory_space=pl.ANY)
        dma = pltpu.SemaphoreType.DMA
        near = pl.BlockSpec(memory_space=pltpu.VMEM)
        hbm = lambda v: pltpu.with_memory_space_constraint(v, pltpu.HBM)
        theta, surface, kappa, depth, wet, ids, counts, weights = map(
            hbm, (theta, surface, kappa, depth, wet, ids.transpose(0, 1, 3, 2), counts, weights)
        )
        fields = pl.pallas_call(
            functools.partial(kernel, n_gx, n_gy),
            out_shape=(
                jax.ShapeDtypeStruct((CX, LEV, CY), F32),
                jax.ShapeDtypeStruct((CX, CY), F32),
            ),
            in_specs=[spec] * 9,
            out_specs=(near, near),
            scratch_shapes=[
                pltpu.VMEM((NSTEP, CX + 2, ROWS, CY), F32),
                pltpu.VMEM((NSTEP, 4, 8, CY), F32),
                pltpu.VMEM((NSTEP, 2, 4, 8, CY), F32),
                pltpu.VMEM((NSTEP, 8, CY), F32),
                pltpu.VMEM((NSTEP, 6, 8, CY), F32),
                pltpu.VMEM((CX + 2, ROWS, CY), F32),
                pltpu.VMEM((2, CX, CY), F32),
                pltpu.VMEM((64, 128), F32),
                pltpu.VMEM((sources, 64, 128), F32),
                pltpu.VMEM((sources * 64, 256), BF16),
                pltpu.VMEM((8, 32, 16, 128), BF16),
                pltpu.VMEM((640, 256), BF16),
                pltpu.VMEM((8, SLOTS, 32), jnp.int32),
                pltpu.VMEM((8, 32), jnp.int32),
                pltpu.VMEM((CX, CY), jnp.int32),
                pltpu.VMEM((11, CX, CY), F32),
                pltpu.VMEM((4, 256, 128), BF16),
                pltpu.VMEM((SLOTS, 256, sources * 64), BF16),
                pltpu.VMEM((2, 4, 8, 128), F32),
                pltpu.VMEM((2, CX, CY), F32),
                pltpu.VMEM((15, CX, CY), F32),
                pltpu.VMEM((14, CX, CY), F32),
                pltpu.VMEM((phases + 1, 8, 128), F32),
                pltpu.VMEM((phases, widest, 8, 128), F32),
                dma((42,)),
                dma((NSTEP, 14)),
                dma((NSTEP, 14)),
                dma((sources,)),
                dma((sources,)),
                dma((phases, widest)),
                dma((phases, widest)),
            ],
            compiler_params=pltpu.CompilerParams(
                collective_id=0, has_side_effects=True, vmem_limit_bytes=36 * 1024 * 1024
            ),
        )(
            theta,
            surface,
            kappa,
            depth,
            wet,
            ids,
            counts,
            weights,
            hbm(jnp.asarray(constants)),
        )
        return pl.pallas_call(
            store_kernel,
            out_shape=(
                jax.ShapeDtypeStruct((1, LEV, CX, CY), F32),
                jax.ShapeDtypeStruct((1, CX, CY), F32),
            ),
            in_specs=[near, near],
            out_specs=(spec, spec),
            scratch_shapes=[dma((CX + 1,))],
            compiler_params=pltpu.CompilerParams(vmem_limit_bytes=8 * 1024 * 1024),
        )(*fields)

    in_specs = (
        P("comp", None, "gx", "gy"),
        P("comp", "gx", "gy"),
        P("comp", "gx", "gy"),
        P("gx", "gy"),
        P("gx", "gy"),
        P("comp", "gx", "gy", None),
        P("comp", "gx", "gy"),
        P("comp", "gx", "gy", None, None),
    )
    out_specs = (P("comp", None, "gx", "gy"), P("comp", "gx", "gy"))
    return jax.shard_map(
        per_device, mesh=mesh, in_specs=in_specs, out_specs=out_specs, check_vma=False
    )
```

```python
import functools

import jax
import jax.numpy as jnp
import ml_dtypes
import numpy as np
from jax import lax
from jax.experimental import pallas as pl
from jax.experimental.pallas import tpu as pltpu
from jax.sharding import PartitionSpec as P

MESH = pl.DeviceIdType.MESH
F32 = jnp.float32
BF16 = jnp.bfloat16

NSTEP = 6
ITERS = 4
SLOTS = 8
LEV = 48
CX = 32
CY = 128
ROWS = 56
SURF = 48
EDGE = (0, 1, 2, 3, 28, 29, 30, 31)
INNER = tuple(range(4, 28))

node_derivative = np.array(
    [
        [-3.0, 4.045084971874737, -1.545084971874737, 0.5],
        [-0.809016994374947, 0.0, 1.118033988749895, -0.309016994374947],
        [0.309016994374947, -1.118033988749895, 0.0, 0.809016994374947],
        [-0.5, 1.545084971874737, -4.045084971874737, 3.0],
    ]
)
second_derivative = node_derivative @ node_derivative
vertical_mix = 0.2
heat_rate = 0.5
air_rate = 0.3
press_rate = 0.1
damping = 0.05
fresh_rate = 0.5
bound_low = 0.02
bound_high = 2.0


def heat_response():
    level = np.zeros(LEV)
    for _ in range(NSTEP):
        change = level[1:] - level[:-1]
        level = level + vertical_mix * (np.append(change, 0.0) - np.append(0.0, change))
        level[0] += heat_rate
    return [float(v) for v in level]


def halves(table):
    high = table.astype(ml_dtypes.bfloat16)
    low = (table - high.astype(np.float64)).astype(ml_dtypes.bfloat16)
    return high, low


def tables():
    lane = np.arange(256)
    f_in, dx_in, dy_in = (lane // 64) % 2, (lane // 16) % 4, lane % 4
    f_out, dx_out, dy_out = lane // 128, (lane // 4) % 4, lane % 4
    fold = (
        (f_in[:, None] == f_out[None])
        & (dx_in[:, None] == dx_out[None])
        & (dy_in[:, None] == dy_out[None])
    )
    block = np.kron(np.eye(32), second_derivative.T)
    high, low = halves(block)
    zero = np.zeros((128, 128))
    lap = np.block(
        [[high.astype(np.float64), low.astype(np.float64)], [high.astype(np.float64), zero]]
    )
    lane = np.arange(128)
    target = ((lane // 4) % 4) * 32 + (lane // 16) * 4 + lane % 4
    perm = np.zeros((128, 256))
    perm[lane, target] = 1.0
    return np.concatenate([fold.astype(np.float64), lap, perm]).astype(ml_dtypes.bfloat16)


def split(value):
    high = value.astype(BF16)
    low = (value - high.astype(F32)).astype(BF16)
    return high, low


def dot(a, b):
    return jnp.dot(a, b, preferred_element_type=F32)


def radices(count):
    if count == 32:
        return [4, 2, 4]
    found = []
    while count > 1:
        size = 4 if count % 4 == 0 else count
        found.append(size)
        count //= size
    return found


def kernel(
    n_gx,
    n_gy,
    theta,
    surface,
    kappa,
    depth,
    wet,
    ids,
    counts,
    weights,
    consts,
    fin,
    surface_fin,
    fp,
    ys,
    yr,
    ye,
    yer,
    yc,
    zb,
    ex,
    tsend,
    trecv,
    table,
    wbuf,
    cbuf,
    idbuf,
    cntbuf,
    wetbuf,
    coef,
    pb,
    hot,
    dbuf,
    imp,
    pcr,
    grid,
    red,
    redr,
    lsem,
    hs,
    hr,
    es,
    er,
    rs,
    rr,
):
    comp = lax.axis_index("comp")
    gx = lax.axis_index("gx")
    gy = lax.axis_index("gy")
    sources = 3 * n_gy
    units = (CX // 4) * (CY // 4)
    is_ocean = comp == 0
    is_air = comp == 1
    has_south = gy > 0
    has_north = gy < n_gy - 1

    def place(dc, dx, dy):
        return (lax.rem(comp + dc, 2), lax.rem(gx + dx + n_gx, n_gx), lax.rem(gy + dy + n_gy, n_gy))

    halo_peers = [
        place(0, 1, 0),
        place(0, -1, 0),
        place(0, 0, 1),
        place(0, 0, -1),
        place(0, 1, 1),
        place(0, -1, 1),
        place(0, 1, -1),
        place(0, -1, -1),
    ]
    export_peers = [(d, j, place(1, d, j)) for d in (-1, 0, 1) for j in range(n_gy)]
    sum_phases = []
    sum_phases.append([place(dc, 0, j) for dc in range(2) for j in range(n_gy) if dc or j])
    stride = 1
    for size in radices(n_gx):
        digit = lax.rem(gx // stride, size)
        group = []
        for j in range(1, size):
            group.append((comp, gx + (lax.rem(digit + j, size) - digit) * stride, gy))
        sum_phases.append(group)
        stride *= size

    barrier = pltpu.get_barrier_semaphore()
    greeted = halo_peers + [p for _, _, p in export_peers] + [p for g in sum_phases for p in g]
    for peer in greeted:
        pl.semaphore_signal(barrier, inc=1, device_id=peer, device_id_type=MESH)

    loads = {}

    def load(name, index, src, dst):
        copy = pltpu.make_async_copy(src, dst, lsem.at[index])
        copy.start()
        loads.setdefault(name, []).append(copy)

    def loaded(name):
        for copy in loads.pop(name):
            copy.wait()

    load("export", 0, theta.at[0, 0], grid.at[0])
    load("export", 1, surface.at[0], grid.at[1])
    load("export", 2, wet, wetbuf)
    load("export", 3, kappa.at[0], grid.at[2])
    load("export", 4, depth, grid.at[3])
    for x in range(CX):
        load("theta", 8 + x, theta.at[0, :, x, :], fp.at[0, x + 1, pl.ds(0, LEV), :])
    load("remap", 5, ids.at[0], idbuf)
    load("remap", 6, counts.at[0], cntbuf)
    load("tables", 7, consts, cbuf)
    load("weights", 40, weights.at[0], wbuf)

    lane128 = lax.broadcasted_iota(jnp.int32, (8, 128), 1)
    lane1 = lax.broadcasted_iota(jnp.int32, (1, 128), 1)

    loaded("export")
    wet_float = wetbuf[...].astype(F32)
    grid[4] = wet_float
    top = grid[0]

    ex[0] = jnp.where(is_ocean, top * wet_float, top)
    ex[1] = jnp.where(is_ocean, wet_float, grid[1])
    parts = [ex[f, pl.ds(dx, 8, stride=4), :] for f in range(2) for dx in range(4)]
    for h in range(8):
        acc = jnp.zeros((8, 128), F32)
        for j in range(8):
            shift = ((j - h) * 16) % 128
            moved = pltpu.roll(parts[j], shift, 1) if shift else parts[j]
            acc = jnp.where(lane128 // 16 == j, moved, acc)
        tsend[pl.ds(8 * h, 8), :] = acc

    for x in range(CX):
        fp[0, x + 1, SURF : SURF + 1, :] = grid[1, x : x + 1, :]
        fp[0, x + 1, SURF + 1 : SURF + 2, :] = grid[2, x : x + 1, :]
        fp[0, x + 1, SURF + 2 : SURF + 3, :] = grid[3, x : x + 1, :]
        fp[0, x + 1, SURF + 3 : SURF + 4, :] = grid[4, x : x + 1, :]
        fp[0, x + 1, SURF + 4 : SURF + 8, :] = jnp.zeros((4, 128), F32)

    def place_in(acc, moved, lane):
        return jnp.where((lane128 == lane) | (lane128 == lane + 1), moved, acc)

    def pack_inner(s, slabs, blocks):
        for j in range(4):
            acc = jnp.zeros((8, 128), F32)
            found = False
            for b in (2 * j, 2 * j + 1):
                if b in blocks:
                    found = True
                    for x in slabs:
                        lane = 2 * x + 64 * (b % 2)
                        moved = pltpu.roll(fp[s, x + 1, 8 * b : 8 * b + 8, :], (lane + 1) % 128, 1)
                        acc = place_in(acc, moved, lane)
            if found:
                ys[s, j] = acc

    def pack_edge(s, blocks):
        acc = jnp.zeros((8, 128), F32)
        for b in blocks:
            for e, x in enumerate(EDGE):
                lane = 16 * b + 2 * e
                moved = pltpu.roll(fp[s, x + 1, 8 * b : 8 * b + 8, :], lane + 1, 1)
                acc = place_in(acc, moved, lane)
        ye[s] = acc

    def pack_corner(s, side, blocks):
        e = 7 * side
        acc = jnp.zeros((8, 128), F32)
        for b in blocks:
            lane = 16 * b + 2 * e
            x = EDGE[e]
            moved = pltpu.roll(fp[s, x + 1, 8 * b : 8 * b + 8, :], lane + 1, 1)
            acc = place_in(acc, moved, lane)
        yc[s, side] = acc

    def merge(low, high):
        return jnp.where(lane128 % 2 == 0, low, pltpu.roll(high, 126, 1))

    def turn(value, lane):
        return pltpu.roll(value, (128 - lane) % 128, 1) if lane % 128 else value

    def unpack_inner(s, slabs, blocks):
        for j in range(4):
            if 2 * j in blocks or 2 * j + 1 in blocks:
                both = merge(yr[s, 0, j], yr[s, 1, j])
                for b in (2 * j, 2 * j + 1):
                    if b in blocks:
                        for x in slabs:
                            zb[x + 1, 8 * b : 8 * b + 8, :] = turn(both, 2 * x + 64 * (b % 2))

    def unpack_edge(s, blocks):
        both = merge(yer[s, 0], yer[s, 1])
        for b in blocks:
            for e, x in enumerate(EDGE):
                zb[x + 1, 8 * b : 8 * b + 8, :] = turn(both, 16 * b + 2 * e)

    def unpack_corner(s, side, blocks):
        both = merge(yer[s, 2 + side], yer[s, 4 + side])
        for b in blocks:
            if side:
                zb[CX + 1, 8 * b : 8 * b + 8, :] = turn(both, 16 * b)
            else:
                zb[0, 8 * b : 8 * b + 8, :] = turn(both, 16 * b + 14)

    def copy_to(s, d):
        peer = halo_peers[d % 2 if d < 4 else 2 + d % 2 if d < 10 else d - 6]
        if d < 4:
            rows = pl.ds(0, LEV) if d < 2 else pl.ds(SURF, 8)
            src = fp.at[s, CX if d % 2 == 0 else 1, rows, :]
            dst = fp.at[s, 0 if d % 2 == 0 else CX + 1, rows, :]
        elif d < 6:
            src, dst = ye.at[s], yer.at[s, d - 4]
        elif d < 8:
            src, dst = ys.at[s, pl.ds(0, 3)], yr.at[s, d - 6, pl.ds(0, 3)]
        elif d < 10:
            src, dst = ys.at[s, 3], yr.at[s, d - 8, 3]
        else:
            src, dst = yc.at[s, 1 - d % 2], yer.at[s, d - 8]
        return pltpu.make_async_remote_copy(
            src_ref=src,
            dst_ref=dst,
            send_sem=hs.at[s, d],
            recv_sem=hr.at[s, d],
            device_id=peer,
            device_id_type=MESH,
        )

    SLAB, SLAB_SURF, OUTER, INSIDE, SURF_COLUMN = (0, 1), (2, 3), (4, 5), (6, 7), (8, 9)
    CORNER = (10, 11, 12, 13)

    def send(s, *kinds):
        for kind in kinds:
            for d in kind:
                copy_to(s, d).start()

    def wait(s, *kinds):
        for kind in kinds:
            for d in kind:
                copy_to(s, d).wait_recv()

    def drain_halo(s):
        kinds = [SLAB, OUTER, INSIDE]
        if s < ITERS:
            kinds += [SLAB_SURF, SURF_COLUMN]
        for kind in kinds:
            for d in kind:
                copy_to(s, d).wait_send()

        @pl.when(is_air)
        def _():
            for d in CORNER:
                copy_to(s, d).wait_send()

    def export_copy(d, j, peer):
        slot = (1 - d) * n_gy + gy
        return pltpu.make_async_remote_copy(
            src_ref=tsend,
            dst_ref=trecv.at[slot],
            send_sem=es.at[(d + 1) * n_gy + j],
            recv_sem=er.at[slot],
            device_id=peer,
            device_id_type=MESH,
        )

    ALL = tuple(range(CX))
    LEVELS = tuple(range(6))
    BOTH = tuple(range(7))
    loaded("theta")
    pack_edge(0, BOTH)
    pack_corner(0, 0, BOTH)
    pack_corner(0, 1, BOTH)
    pack_inner(0, INNER, LEVELS)
    pack_inner(0, ALL, (6,))
    pl.semaphore_wait(barrier, len(greeted))

    @pl.when(is_air)
    def _():
        send(0, CORNER)

    send(0, SLAB, SLAB_SURF, OUTER, INSIDE, SURF_COLUMN)
    for d, j, peer in export_peers:
        if d:
            export_copy(d, j, peer).start()
    for d, j, peer in export_peers:
        if not d:
            export_copy(d, j, peer).start()

    loaded("remap")
    loaded("tables")
    gy_bits = n_gy.bit_length() - 1
    id_all = idbuf[...]
    unit = id_all & (units - 1)
    dev = id_all >> 8
    dev_gy = dev & (n_gy - 1)
    offset = (dev >> gy_bits) - gx + 1
    offset = jnp.where(offset < 0, offset + n_gx, jnp.where(offset >= n_gx, offset - n_gx, offset))
    tile_y = unit & 31
    source = offset * n_gy + dev_gy
    row = (tile_y >> 2) * 8 + (unit >> 5)
    low_tile = tile_y & 3
    slot_order = lax.broadcasted_iota(jnp.int32, (8, SLOTS, 32), 1)
    source = jnp.where(slot_order < cntbuf[...][:, None, :], source, 200)
    eye = jnp.where(
        lax.broadcasted_iota(jnp.int32, (32, 32), 0) == lax.broadcasted_iota(jnp.int32, (32, 32), 1),
        1.0,
        0.0,
    ).astype(BF16)
    columns = []
    for tx in range(8):
        stacked = jnp.concatenate([source[tx], row[tx], low_tile[tx], low_tile[tx]], axis=0)
        columns.append(
            lax.dot_general(
                eye,
                stacked.astype(F32).astype(BF16),
                (((1,), (1,)), ((), ())),
                preferred_element_type=F32,
            )
        )
    columns = jnp.concatenate(columns, axis=0)
    key = columns[:, 0:8] * 64.0 + columns[:, 8:16]
    tile_low = columns[:, 16:24]
    key_lane = lax.broadcasted_iota(jnp.int32, (units, sources * 64), 1).astype(F32)
    for m in range(SLOTS):
        hot[m] = jnp.where(key[:, m : m + 1] == key_lane, 1.0, 0.0).astype(BF16)

    wait(0, INSIDE, OUTER, SURF_COLUMN)
    unpack_inner(0, INNER, LEVELS)
    unpack_inner(0, ALL, (6,))
    unpack_edge(0, LEVELS)
    wait(0, SLAB, SLAB_SURF)

    @pl.when(is_air)
    def _():
        wait(0, CORNER)
        unpack_corner(0, 0, BOTH)
        unpack_corner(0, 1, BOTH)


    def lanes_of(shape):
        return lax.broadcasted_iota(jnp.int32, shape, 1)

    lane_full = lanes_of((CX, CY))

    def gather_row(s, row, slot):
        for x in range(CX):
            grid[slot, x : x + 1, :] = fp[s, x + 1, row : row + 1, :]

    def rim_row(row, slot):
        for x in range(CX):
            grid[slot, x : x + 1, :] = zb[x + 1, row : row + 1, :]

    def shifted(center, west_row, east_row, rim):
        row_place = lax.broadcasted_iota(jnp.int32, (CX, CY), 0)
        east = jnp.where(row_place == CX - 1, east_row, pltpu.roll(center, CX - 1, 0))
        west = jnp.where(row_place == 0, west_row, pltpu.roll(center, 1, 0))
        north = jnp.where(lane_full == CY - 1, rim, pltpu.roll(center, CY - 1, 1))
        south = jnp.where(lane_full == 0, rim, pltpu.roll(center, 1, 1))
        return east, west, north, south

    def side_rows(s, row):
        return fp[s, 0, row : row + 1, :], fp[s, CX + 1, row : row + 1, :]

    def wet_sides():
        wet_c = grid[4]
        rim_row(SURF + 3, 5)
        we, ww, wn, ws = shifted(wet_c, *side_rows(0, SURF + 3), grid[5])
        wn = jnp.where((lane_full == CY - 1) & jnp.logical_not(has_north), 0.0, wn)
        ws = jnp.where((lane_full == 0) & jnp.logical_not(has_south), 0.0, ws)
        return wet_c, we, ww, wn, ws

    def faces(row, slot, at):
        wet_c, we, ww, wn, ws = wet_sides()
        center = grid[slot]
        rim_row(row, 5)
        ke, kw, kn, ks = shifted(center, *side_rows(0, row), grid[5])
        base = center * wet_c
        coef[at] = 0.5 * (base + ke * we) * wet_c * we
        coef[at + 1] = 0.5 * (kw * ww + base) * ww * wet_c
        coef[at + 2] = 0.5 * (base + kn * wn) * wet_c * wn
        coef[at + 3] = 0.5 * (ks * ws + base) * ws * wet_c

    @pl.when(is_ocean)
    def _():
        faces(SURF + 1, 2, 0)
        wet_c = grid[4]
        coef[4] = (
            1.0 - (coef[0] + coef[1] + coef[2] + coef[3]) - (2.0 * vertical_mix) * wet_c
        )
        coef[5] = vertical_mix * wet_c

    def line_factors():
        faces(SURF + 2, 3, 6)
        wet_c = grid[4]
        diagonal = damping + coef[6] + coef[7] + coef[8] + coef[9]
        coef[10] = diagonal
        main = wet_c * diagonal + (1.0 - wet_c)
        lower = jnp.where(lane_full == 0, 0.0, -coef[9])
        upper = jnp.where(lane_full == CY - 1, 0.0, -coef[8])
        step = 1
        index = 0
        while step < CY:
            back = CY - step
            below_main = pltpu.roll(main, step, 1)
            above_main = pltpu.roll(main, back, 1)
            factor_below = -lower / below_main
            factor_above = -upper / above_main
            pcr[index] = factor_below
            pcr[index + 1] = factor_above
            main = (
                main
                + factor_below * pltpu.roll(upper, step, 1)
                + factor_above * pltpu.roll(lower, back, 1)
            )
            lower = factor_below * pltpu.roll(lower, step, 1)
            upper = factor_above * pltpu.roll(upper, back, 1)
            step *= 2
            index += 2
        pcr[14] = 1.0 / main

    def solve(values):
        step = 1
        index = 0
        while step < CY:
            values = (
                values
                + pcr[index] * pltpu.roll(values, step, 1)
                + pcr[index + 1] * pltpu.roll(values, CY - step, 1)
            )
            step *= 2
            index += 2
        return values * pcr[14]

    row48 = lax.broadcasted_iota(jnp.int32, (LEV, CY), 0)
    lane48 = lanes_of((LEV, CY))

    def out_ref(s, x):
        return fin.at[x] if s == NSTEP else fp.at[s, x + 1]

    def ocean_step(s, slabs):
        for x in slabs:
            c = fp[s - 1, x + 1, 0:LEV, :]
            w = fp[s - 1, x, 0:LEV, :]
            e = fp[s - 1, x + 2, 0:LEV, :]
            z = zb[x + 1, 0:LEV, :]

            def row(i, x=x):
                return coef[i, x : x + 1, :]

            n = jnp.where(lane48 == CY - 1, z, pltpu.roll(c, CY - 1, 1))
            o = jnp.where(lane48 == 0, z, pltpu.roll(c, 1, 1))
            up = jnp.where(row48 == LEV - 1, c, pltpu.roll(c, LEV - 1, 0))
            down = jnp.where(row48 == 0, c, pltpu.roll(c, 1, 0))
            new = (
                row(4) * c
                + row(0) * e
                + row(1) * w
                + row(2) * n
                + row(3) * o
                + row(5) * (up + down)
            )
            out_ref(s, x)[0:LEV, :] = new
            if s > 1:
                out_ref(s, x)[0:1, :] = new[0:1, :] + grid[7, x : x + 1, :]

    def air_step(s, tiles):
        rows = ROWS if s <= ITERS else LEV
        lane_r = lanes_of((rows, CY))
        row_r = lax.broadcasted_iota(jnp.int32, (rows, CY), 0)
        h = jnp.where(
            ((lane1 % 4 == 0) & ((lane1 > 0) | has_south))
            | ((lane1 % 4 == 3) & ((lane1 < CY - 1) | has_north)),
            0.5,
            0.0,
        )
        mix_up = jnp.where(row_r < LEV - 1, vertical_mix, 0.0)
        mix_down = jnp.where((row_r > 0) & (row_r < LEV), vertical_mix, 0.0)

        for i in tiles:
            x0 = 4 * i
            v = [fp[s - 1, x0 + j, 0:rows, :] for j in range(6)]
            z = [zb[x0 + j, 0:rows, :] for j in range(6)]

            def across(t):
                return [0.5 * (t[1] + t[0]), t[2], t[3], 0.5 * (t[4] + t[5])]

            blocks = []
            for a, za in zip(across(v), across(z)):
                partner = jnp.where(lane_r % 4 == 0, pltpu.roll(a, 1, 1), pltpu.roll(a, CY - 1, 1))
                partner = jnp.where((lane_r == 0) | (lane_r == CY - 1), za, partner)
                blocks.append(a + h * (partner - a))
            high, low = split(jnp.concatenate(blocks, axis=0))
            along = dot(jnp.concatenate([high, low], axis=1), cbuf[256:512, :])
            along = along[:, :CY] + along[:, CY:]
            for j in range(4):
                b = blocks[j]
                lap = along[rows * j : rows * (j + 1)]
                for m in range(4):
                    lap = lap + float(second_derivative[j, m]) * blocks[m]
                up = pltpu.roll(b, rows - 1, 0)
                down = pltpu.roll(b, 1, 0)
                new = (
                    b
                    + grid[2, x0 + j : x0 + j + 1, :] * lap
                    + mix_up * (up - b)
                    + mix_down * (down - b)
                )
                x = x0 + j
                out_ref(s, x)[0:rows, :] = new
                if s == 1:
                    grid[8, x : x + 1, :] = b[0:1, :]
                    grid[9, x : x + 1, :] = b[SURF : SURF + 1, :]
                else:
                    out_ref(s, x)[0:1, :] = (
                        new[0:1, :]
                        + grid[6, x : x + 1, :]
                        - grid[7, x : x + 1, :] * b[0:1, :]
                    )
                    if s <= ITERS:
                        fp[s, x + 1, SURF : SURF + 1, :] = (
                            new[SURF : SURF + 1, :]
                            + grid[10, x : x + 1, :]
                            - press_rate * b[SURF : SURF + 1, :]
                        )


    def apply_a(s, center):
        wet_c = grid[4]
        rim_row(SURF, 5)
        east, west, north, south = shifted(center, *side_rows(s, SURF), grid[5])
        near = coef[6] * east + coef[7] * west + coef[8] * north + coef[9] * south
        return wet_c * (coef[10] * center - near) + (1.0 - wet_c) * center

    @pl.when(is_ocean)
    def _():
        ocean_step(1, ALL)
        line_factors()
        grid[8] = apply_a(0, grid[1])

    @pl.when(is_air)
    def _():
        unpack_edge(0, (6,))
        air_step(1, tuple(range(CX // 4)))

    for d in range(3):
        for j in range(n_gy):
            slot = d * n_gy + j
            pltpu.make_async_remote_copy(
                src_ref=tsend,
                dst_ref=trecv.at[slot],
                send_sem=es.at[slot],
                recv_sem=er.at[slot],
                device_id=halo_peers[0],
                device_id_type=MESH,
            ).wait_recv()
    high, low = split(trecv[...].reshape(sources * 64, 128))
    table[:, 0:128] = high
    table[:, 128:256] = low
    lane256 = lax.broadcasted_iota(jnp.int32, (units, 256), 1)
    low_lane = ((lane256 // 4) % 4).astype(F32)
    slot_of = (lane256 // 16) % 8
    picked = jnp.zeros((units, 256), F32)
    for m in range(SLOTS):
        found = dot(hot[m], table[...])
        found = jnp.where(low_lane == tile_low[:, m : m + 1], found, 0.0).astype(BF16)
        picked = jnp.where(slot_of == m, dot(found, cbuf[0:256, :]), picked)
    high, low = split(picked)
    pb[0] = high[:, 0:128]
    pb[1] = high[:, 128:256]
    pb[2] = low[:, 0:128]
    pb[3] = low[:, 128:256]
    loaded("weights")
    own_tile = lax.broadcasted_iota(jnp.int32, (16, 256), 0) == (
        lax.broadcasted_iota(jnp.int32, (16, 256), 1) // 16
    )
    for g in range(16):
        left = pb[:, 16 * g : 16 * g + 16, :].reshape(64, 128)
        right = wbuf[g // 2, 16 * (g % 2) : 16 * (g % 2) + 16].reshape(256, 128)
        out = lax.dot_general(
            left, right, (((1,), (1,)), ((), ())), preferred_element_type=F32
        )
        for f in range(2):
            value = out[16 * f : 16 * f + 16] + out[32 + 16 * f : 48 + 16 * f]
            value = jnp.sum(jnp.where(own_tile, value, 0.0), axis=0, keepdims=True)
            for u in range(2):
                dbuf[f, 2 * (g % 2) + u, g // 2 : g // 2 + 1, :] = value[:, 128 * u : 128 * u + 128]
    high, low = split(dbuf[...].reshape(64, 128))
    turned = dot(jnp.concatenate([high, low], axis=0), cbuf[512:640, 0:128])
    turned = turned[:64] + turned[64:]
    for f in range(2):
        quarters = [turned[32 * f + 8 * q : 32 * f + 8 * q + 8] for q in range(4)]
        for dx in range(4):
            acc = jnp.zeros((8, 128), F32)
            for q in range(4):
                shift = ((q - dx) * 32) % 128
                moved = pltpu.roll(quarters[q], shift, 1) if shift else quarters[q]
                acc = jnp.where(lane128 // 32 == q, moved, acc)
            imp[f, pl.ds(dx, 8, stride=4), :] = acc

    wet_c = grid[4]
    heat = jnp.where(is_ocean, -(wet_c * imp[0]), grid[0])
    cells = jnp.where(is_ocean, wet_c, 0.0)
    row8 = lax.broadcasted_iota(jnp.int32, (8, 128), 0)

    def rows8(v):
        return jnp.sum(v, axis=0, keepdims=True)

    red[0] = jnp.where(row8 == 0, rows8(heat), jnp.where(row8 == 1, rows8(cells), 0.0))

    def sum_copy(phase, j):
        return pltpu.make_async_remote_copy(
            src_ref=red.at[phase],
            dst_ref=redr.at[phase, j],
            send_sem=rs.at[phase, j],
            recv_sem=rr.at[phase, j],
            device_id=sum_phases[phase][j],
            device_id_type=MESH,
        )

    def sum_send(phase):
        for j in range(len(sum_phases[phase])):
            sum_copy(phase, j).start()

    def sum_finish(phase):
        total = red[phase]
        for j in range(len(sum_phases[phase])):
            sum_copy(phase, j).wait_recv()
            total = total + redr[phase, j]
        red[phase + 1] = total

    sum_send(0)

    centre = (bound_high + bound_low) / 2.0
    half_range = (bound_high - bound_low) / 2.0
    spread_ratio = centre / half_range

    def put_surface(s, value):
        grid[13] = value
        if s < ITERS:
            for x in range(CX):
                fp[s, x + 1, SURF : SURF + 1, :] = grid[13, x : x + 1, :]

    @pl.when(is_ocean)
    def _():
        force = heat_rate * wet_c * imp[0]
        grid[7] = force
        for x in range(CX):
            fp[1, x + 1, 0:1, :] = fp[1, x + 1, 0:1, :] + grid[7, x : x + 1, :]
        send(1, SLAB)
        pack_edge(1, LEVELS)
        send(1, OUTER)
        pack_inner(1, INNER, LEVELS)
        send(1, INSIDE)
        eta = grid[1]
        residual = wet_c * (damping * eta + fresh_rate * imp[1]) - grid[8]
        direction = solve(residual) / centre
        grid[11] = eta + direction
        grid[12] = residual
        put_surface(1, direction)
        send(1, SLAB_SURF)
        pack_inner(1, ALL, (6,))
        send(1, SURF_COLUMN)

    @pl.when(is_air)
    def _():
        grid[6] = air_rate * imp[0]
        grid[7] = air_rate * imp[1]
        grid[10] = press_rate * imp[0]
        grid[5] = grid[6] - grid[7] * grid[8]
        grid[11] = grid[10] - press_rate * grid[9]
        for x in range(CX):
            fp[1, x + 1, 0:1, :] = fp[1, x + 1, 0:1, :] + grid[5, x : x + 1, :]
            fp[1, x + 1, SURF : SURF + 1, :] = (
                fp[1, x + 1, SURF : SURF + 1, :] + grid[11, x : x + 1, :]
            )
        pack_corner(1, 0, BOTH)
        pack_corner(1, 1, BOTH)
        send(1, CORNER, SLAB, SLAB_SURF)
        pack_edge(1, BOTH)
        send(1, OUTER)
        pack_inner(1, INNER, BOTH)
        send(1, INSIDE, SURF_COLUMN)

    recurrence = 1.0 / spread_ratio
    phases = len(sum_phases)
    for s in range(2, NSTEP + 1):
        last = s == NSTEP
        recurrence_next = 1.0 / (2.0 * spread_ratio - recurrence)

        @pl.when(is_ocean)
        def _(s=s, last=last, recurrence=recurrence, recurrence_next=recurrence_next):
            wait(s - 1, INSIDE)
            unpack_inner(s - 1, INNER, LEVELS)
            ocean_step(s, INNER)
            if not last:
                pack_inner(s, INNER, LEVELS)
                send(s, INSIDE)
            if s <= ITERS:
                wait(s - 1, SURF_COLUMN, SLAB_SURF)
                unpack_inner(s - 1, ALL, (6,))
                old = grid[13]
                residual = grid[12] - apply_a(s - 1, old)
                direction = (recurrence_next * recurrence) * old + (
                    2.0 * recurrence_next / half_range
                ) * solve(residual)
                grid[11] = grid[11] + direction
                grid[12] = residual
                put_surface(s, direction)
                if s < ITERS:
                    send(s, SLAB_SURF)
                    pack_inner(s, ALL, (6,))
                    send(s, SURF_COLUMN)
            wait(s - 1, OUTER)
            unpack_edge(s - 1, LEVELS)
            ocean_step(s, EDGE[1:-1])
            for side, x in ((0, 0), (1, CX - 1)):
                wait(s - 1, (side,))
                ocean_step(s, (x,))
                if not last:
                    send(s, (1 - side,))
            if not last:
                pack_edge(s, LEVELS)
                send(s, OUTER)

        @pl.when(is_air)
        def _(s=s, last=last):
            used = BOTH if s <= ITERS else LEVELS
            made = BOTH if s < ITERS else LEVELS
            wait(s - 1, INSIDE, OUTER)
            if s <= ITERS:
                wait(s - 1, SURF_COLUMN)
            unpack_inner(s - 1, INNER, used)
            unpack_edge(s - 1, used)
            air_step(s, tuple(range(1, CX // 4 - 1)))
            if not last:
                pack_inner(s, INNER, made)
                send(s, INSIDE)
                if s < ITERS:
                    send(s, SURF_COLUMN)
            for side in (0, 1):
                wait(s - 1, (side,), (10 + side, 12 + side))
                if s <= ITERS:
                    wait(s - 1, (2 + side,))
                unpack_corner(s - 1, side, used)
            air_step(s, (0, CX // 4 - 1))
            if not last:
                pack_corner(s, 0, made)
                pack_corner(s, 1, made)
                send(s, CORNER, SLAB)
                if s < ITERS:
                    send(s, SLAB_SURF)
                pack_edge(s, made)
                send(s, OUTER)
            if s == ITERS:
                gather_row(s, SURF, 11)

        recurrence = recurrence_next
        phase = s - 2
        if phase < phases:
            sum_finish(phase)
            if phase + 1 < phases:
                sum_send(phase + 1)

    total = red[phases]
    correction = jnp.sum(total[0:1, :], axis=1, keepdims=True) / jnp.sum(
        total[1:2, :], axis=1, keepdims=True
    )
    response = heat_response()

    @pl.when(is_ocean)
    def _():
        spread = jnp.zeros((8, 128), F32)
        for k in range(NSTEP):
            spread = jnp.where(row8 == k, response[k], spread)
        spread = spread * correction

        for x in range(CX):
            fin[x, 0:8, :] = fin[x, 0:8, :] + spread * grid[4, x : x + 1, :]

    surface_fin[...] = grid[11]
    for s in range(NSTEP):
        drain_halo(s)
    for d, j, peer in export_peers:
        export_copy(d, j, peer).wait_send()
    for phase in range(phases):
        for j in range(len(sum_phases[phase])):
            sum_copy(phase, j).wait_send()


def store_kernel(fin, surface_fin, theta_out, surface_out, sem):
    copies = [pltpu.make_async_copy(surface_fin, surface_out.at[0], sem.at[CX])]
    for x in range(CX):
        copies.append(pltpu.make_async_copy(fin.at[x], theta_out.at[0, :, x, :], sem.at[x]))
    for copy in copies:
        copy.start()
    for copy in copies:
        copy.wait()


def solution(mesh):
    n_gx = mesh.shape["gx"]
    n_gy = mesh.shape["gy"]
    sources = 3 * n_gy
    phases = 1 + len(radices(n_gx))
    widest = max(2 * n_gy - 1, 3)
    constants = tables()

    def per_device(theta, surface, kappa, depth, wet, ids, counts, weights):
        spec = pl.BlockSpec(memory_space=pl.ANY)
        dma = pltpu.SemaphoreType.DMA
        near = pl.BlockSpec(memory_space=pltpu.VMEM)
        hbm = lambda v: pltpu.with_memory_space_constraint(v, pltpu.HBM)
        theta, surface, kappa, depth, wet, ids, counts, weights = map(
            hbm, (theta, surface, kappa, depth, wet, ids.transpose(0, 1, 3, 2), counts, weights)
        )
        fields = pl.pallas_call(
            functools.partial(kernel, n_gx, n_gy),
            out_shape=(
                jax.ShapeDtypeStruct((CX, LEV, CY), F32),
                jax.ShapeDtypeStruct((CX, CY), F32),
            ),
            in_specs=[spec] * 9,
            out_specs=(near, near),
            scratch_shapes=[
                pltpu.VMEM((NSTEP, CX + 2, ROWS, CY), F32),
                pltpu.VMEM((NSTEP, 4, 8, CY), F32),
                pltpu.VMEM((NSTEP, 2, 4, 8, CY), F32),
                pltpu.VMEM((NSTEP, 8, CY), F32),
                pltpu.VMEM((NSTEP, 6, 8, CY), F32),
                pltpu.VMEM((NSTEP, 2, 8, CY), F32),
                pltpu.VMEM((CX + 2, ROWS, CY), F32),
                pltpu.VMEM((2, CX, CY), F32),
                pltpu.VMEM((64, 128), F32),
                pltpu.VMEM((sources, 64, 128), F32),
                pltpu.VMEM((sources * 64, 256), BF16),
                pltpu.VMEM((8, 32, 16, 128), BF16),
                pltpu.VMEM((640, 256), BF16),
                pltpu.VMEM((8, SLOTS, 32), jnp.int32),
                pltpu.VMEM((8, 32), jnp.int32),
                pltpu.VMEM((CX, CY), jnp.int32),
                pltpu.VMEM((11, CX, CY), F32),
                pltpu.VMEM((4, 256, 128), BF16),
                pltpu.VMEM((SLOTS, 256, sources * 64), BF16),
                pltpu.VMEM((2, 4, 8, 128), F32),
                pltpu.VMEM((2, CX, CY), F32),
                pltpu.VMEM((15, CX, CY), F32),
                pltpu.VMEM((14, CX, CY), F32),
                pltpu.VMEM((phases + 1, 8, 128), F32),
                pltpu.VMEM((phases, widest, 8, 128), F32),
                dma((42,)),
                dma((NSTEP, 14)),
                dma((NSTEP, 14)),
                dma((sources,)),
                dma((sources,)),
                dma((phases, widest)),
                dma((phases, widest)),
            ],
            compiler_params=pltpu.CompilerParams(
                collective_id=0, has_side_effects=True, vmem_limit_bytes=36 * 1024 * 1024
            ),
        )(
            theta,
            surface,
            kappa,
            depth,
            wet,
            ids,
            counts,
            weights,
            hbm(jnp.asarray(constants)),
        )
        return pl.pallas_call(
            store_kernel,
            out_shape=(
                jax.ShapeDtypeStruct((1, LEV, CX, CY), F32),
                jax.ShapeDtypeStruct((1, CX, CY), F32),
            ),
            in_specs=[near, near],
            out_specs=(spec, spec),
            scratch_shapes=[dma((CX + 1,))],
            compiler_params=pltpu.CompilerParams(vmem_limit_bytes=8 * 1024 * 1024),
        )(*fields)

    in_specs = (
        P("comp", None, "gx", "gy"),
        P("comp", "gx", "gy"),
        P("comp", "gx", "gy"),
        P("gx", "gy"),
        P("gx", "gy"),
        P("comp", "gx", "gy", None),
        P("comp", "gx", "gy"),
        P("comp", "gx", "gy", None, None),
    )
    out_specs = (P("comp", None, "gx", "gy"), P("comp", "gx", "gy"))
    return jax.shard_map(
        per_device, mesh=mesh, in_specs=in_specs, out_specs=out_specs, check_vma=False
    )
```
